128 devices in a mesh: grp: 2 (over x_hi), gx: 16 (over z, y), gy: 4 (over x_lo, core).
Axes of the slice: x: 4 (x_hi: 2, x_lo: 2; x = x_hi * 2 + x_lo), y: 4, z: 4, core: 2. Of those that a mesh axis runs over, the one named last changes fastest.
Arguments:
- tracers: float32 [256, 1024, 1536], P('grp', 'gx', 'gy'), may hold values from -6 to 6
- dycore_air_mass: float32 [512, 16, 384], P(('grp', 'gx', 'gy')), may hold values from 1 to 2
- dycore_face_flux: float32 [512, 2, 16, 384], P(('grp', 'gx', 'gy')), may hold values from -0.2 to 0.2
- tile_dycore_slot: int32 [256], replicated, may hold values from 0 to 511, as said below
- water_idx: int32 [6], replicated, may hold values from 0 to 255, as said below
Outputs:
- new_tracers: float32 [256, 1024, 1536], P('grp', 'gx', 'gy')
- water_to_dycore: float32 [512, 6, 16, 384], P(('grp', 'gx', 'gy'))
The draws below stay inside these ranges and needn't reach their ends.
Inputs may be any that keep to these rules, and one draw needn't show every extreme that they name: `tile_dycore_slot`: slot g lies on dycore device g // 4, devices in the order grp, gx, gy. Entries are distinct; a device's tiles fill its first slots in the order of the tiles. The tiles of block b lie on distinct dycore devices whose gx index is b // 4; in every gx index some device holds 4 tiles. `water_idx`: distinct tracer numbers; 0 and 255 are always among them.
All inputs are finite; a program needn't handle non-finite values.
Results may differ from the reference program's by a relative error of at most 0.0003.
Values sent between devices are 32-bit elements; how exact they have to be, the bound alone decides.
A program may use at most 256 MiB of HBM per device.

```python
import jax
import jax.numpy as jnp
from jax import lax

NTR = 256
WATER_COUNT = 6
BLOCK_CELLS_Y = 384
TPB = 4
NSUB = 2
TILE_ROWS_X = 16
CAPD = 4
NBLK = 64
NTILE = 256
TILE_SLOT_COUNT = 512
NX = 1024
NY = 1536
N_GRP = 2
N_GX = 16
N_GY = 4


def draw_tile_dycore_slot(key, part):
    group_size = N_GRP * N_GY
    key_hub = jax.random.fold_in(key, 101)
    key_rest = jax.random.fold_in(key, 202)
    key_place = jax.random.fold_in(key, 303)
    hubs = jax.random.randint(key_hub, (N_GX,), 0, group_size, dtype=jnp.int32)
    rest_keys = jax.random.split(key_rest, NBLK)
    place_keys = jax.random.split(key_place, NBLK)
    others = jax.vmap(lambda kk: jax.random.permutation(kk, group_size - 1).astype(jnp.int32))(rest_keys)[:, :TPB - 1]
    places = jax.vmap(lambda kk: jax.random.permutation(kk, TPB).astype(jnp.int32))(place_keys)
    blocks = jnp.arange(NBLK, dtype=jnp.int32)
    column = blocks // N_GY
    block_hub = jnp.take(hubs, column)
    others = others + (others >= block_hub[:, None]).astype(jnp.int32)
    chosen = jnp.concatenate([block_hub[:, None], others], axis=1)
    chosen = jnp.take_along_axis(chosen, places, axis=1)
    local_half = chosen // N_GY
    local_col = chosen % N_GY
    owners = (local_half * (N_GX * N_GY) + column[:, None] * N_GY + local_col).reshape(-1).astype(jnp.int32)
    same = owners[:, None] == owners[None, :]
    tile_ids = jnp.arange(NTILE, dtype=jnp.int32)
    earlier = tile_ids[None, :] < tile_ids[:, None]
    ranks = jnp.sum(same & earlier, axis=1).astype(jnp.int32)
    return (owners * CAPD + ranks).astype(jnp.int32)


def draw_water_idx(key, part):
    key_water = jax.random.fold_in(key, 404)
    key_order = jax.random.fold_in(key, 505)
    middle = jax.random.permutation(key_water, NTR - 2)[:WATER_COUNT - 2].astype(jnp.int32) + 1
    ends = jnp.array([0, NTR - 1], dtype=jnp.int32)
    chosen = jnp.concatenate([ends, middle])
    order = jax.random.permutation(key_order, WATER_COUNT).astype(jnp.int32)
    return jnp.take(chosen, order).astype(jnp.int32)


def block_levels(rng, dims, cuts, smallest, top_value):
    def one(position, shards_of):
        steps = jax.random.uniform(jax.random.fold_in(jax.random.fold_in(rng, 6), position), (shards_of,), jnp.float32, smallest / len(cuts), top_value / len(cuts))
        return jnp.repeat(jnp.exp(steps), dims[position] // shards_of).reshape((-1,) + (1,) * (len(dims) - position - 1))

    gain = one(*cuts[0])
    for cut in cuts[1:]:
        gain = gain * one(*cut)
    return gain


def scatter_about(stream_key, shape, scale, reach, cuts=(), kind=jnp.bfloat16):
    gain = block_levels(stream_key, shape, cuts, -0.22, 0.18) if cuts else 1.0
    values = jax.random.normal(stream_key, shape, jnp.float32) * scale * gain
    return jnp.minimum(jnp.maximum(values, -reach), reach).astype(kind)


def setup_inputs(seed: int = 0) -> dict:
    streams_of = jax.random.split(jax.random.key(seed), 6)
    tracers = scatter_about(streams_of[0], (NTR, NX, NY), 1.0, 6.0, ((0, 2), (1, 16), (2, 4)), jnp.float32)
    dycore_air_mass = jnp.clip(1.0 + 1.0 * jax.random.uniform(streams_of[1], (TILE_SLOT_COUNT, TILE_ROWS_X, BLOCK_CELLS_Y), jnp.float32) ** block_levels(streams_of[1], (TILE_SLOT_COUNT, TILE_ROWS_X, BLOCK_CELLS_Y), ((0, 128),), -0.2, 0.2), 1.0, 2.0)
    dycore_face_flux = jnp.clip(jax.random.uniform(streams_of[2], (TILE_SLOT_COUNT, 2, TILE_ROWS_X, BLOCK_CELLS_Y), jnp.float32, -0.2, 0.2) * block_levels(streams_of[2], (TILE_SLOT_COUNT, 2, TILE_ROWS_X, BLOCK_CELLS_Y), ((0, 128),), -0.4, 0.0), -0.2, 0.2)
    tile_dycore_slot = draw_tile_dycore_slot(jax.random.fold_in(streams_of[5], 71), 0)
    water_idx = draw_water_idx(jax.random.fold_in(streams_of[5], 71), 0)
    return dict(tracers=tracers, dycore_air_mass=dycore_air_mass, dycore_face_flux=dycore_face_flux, tile_dycore_slot=tile_dycore_slot, water_idx=water_idx)


def upwind_faces(behind_one, centre, ahead_one, ahead_two, flow):
    from_left = (-behind_one + 5.0 * centre + 2.0 * ahead_one) / 6.0
    from_right = (2.0 * centre + 5.0 * ahead_one - ahead_two) / 6.0
    return flow * jnp.where(flow > 0, from_left, from_right)


def mass_update(flow_x_pad, flow_y_pad, air_mass):
    cells_x, cells_y = air_mass.shape
    east = flow_x_pad[1:cells_x + 2, 2:cells_y + 2]
    north = flow_y_pad[2:cells_x + 2, 1:cells_y + 2]
    return air_mass - (east[1:] - east[:-1]) - (north[:, 1:] - north[:, :-1])


def advance(padded, flow_x_pad, flow_y_pad, air_mass, mass_next):
    cells_x, cells_y = air_mass.shape
    along_x = padded[:, :, 2:cells_y + 2]
    east = flow_x_pad[1:cells_x + 2, 2:cells_y + 2]
    flux_x = upwind_faces(along_x[:, 0:cells_x + 1], along_x[:, 1:cells_x + 2], along_x[:, 2:cells_x + 3], along_x[:, 3:cells_x + 4], east)
    along_y = padded[:, 2:cells_x + 2, :]
    north = flow_y_pad[2:cells_x + 2, 1:cells_y + 2]
    flux_y = upwind_faces(along_y[:, :, 0:cells_y + 1], along_y[:, :, 1:cells_y + 2], along_y[:, :, 2:cells_y + 3], along_y[:, :, 3:cells_y + 4], north)
    centre = padded[:, 2:cells_x + 2, 2:cells_y + 2]
    return (air_mass * centre - (flux_x[:, 1:] - flux_x[:, :-1]) - (flux_y[:, :, 1:] - flux_y[:, :, :-1])) / mass_next


def to_grid(pieces):
    channels = pieces.shape[1]
    shaped = pieces.reshape(N_GX, N_GY, TPB, channels, TILE_ROWS_X, BLOCK_CELLS_Y)
    return shaped.transpose(3, 0, 2, 4, 1, 5).reshape(channels, NX, NY)


def to_pieces(grid):
    channels = grid.shape[0]
    shaped = grid.reshape(channels, N_GX, TPB, TILE_ROWS_X, N_GY, BLOCK_CELLS_Y)
    return shaped.transpose(1, 4, 2, 0, 3, 5).reshape(NTILE, channels, TILE_ROWS_X, BLOCK_CELLS_Y)


def reference(tracers, dycore_air_mass, dycore_face_flux, tile_dycore_slot, water_idx):
    packed = jnp.concatenate([dycore_air_mass[:, None], dycore_face_flux], axis=1)
    fields = to_grid(jnp.take(packed, tile_dycore_slot, axis=0))
    air_mass = fields[0]
    flows = fields[1:] / NSUB
    flow_pad = jnp.pad(flows, ((0, 0), (2, 2), (2, 2)))
    bundles = tracers.reshape(NTR // 16, 16, NX, NY)
    for substep in range(NSUB):
        mass_next = mass_update(flow_pad[0], flow_pad[1], air_mass)

        def evolve(bundle, old_mass=air_mass, new_mass=mass_next):
            padded = jnp.pad(bundle, ((0, 0), (2, 2), (2, 2)))
            return advance(padded, flow_pad[0], flow_pad[1], old_mass, new_mass)

        bundles = lax.map(evolve, bundles)
        air_mass = mass_next
    mixing = bundles.reshape(NTR, NX, NY)
    water_tracers = to_pieces(jnp.take(mixing, water_idx, axis=0))
    water_to_dycore = jnp.zeros((TILE_SLOT_COUNT, WATER_COUNT, TILE_ROWS_X, BLOCK_CELLS_Y), jnp.float32).at[tile_dycore_slot].set(water_tracers)
    return mixing, water_to_dycore
```

```python
import jax
import jax.numpy as jnp
import numpy as np
from jax import lax
from jax.experimental import pallas as pl
from jax.experimental.pallas import tpu as pltpu
from jax.sharding import PartitionSpec as P

MESH = pl.DeviceIdType.MESH
f32 = jnp.float32
bf16 = jnp.bfloat16

NG, NX, NY = 2, 16, 4
GROUP = NG * NY
TPB = 4
SLOTS = 4
ROWS = 16
J = 3
T = 8
NT = 128
CH = NT // T
NW = 6
PW = 5
EDGE = T * J * 2


def stencil_weights():
    w = np.zeros((256, 256), np.float32)
    for b, taps in enumerate(({-1: -1, 0: 5, 1: 2}, {0: 2, 1: 5, 2: -1})):
        for n in range(128):
            for d, v in taps.items():
                y = n + d
                if 0 <= y < 128:
                    w[y, b * 128 + n] += v
                    if 2 <= y < 126:
                        w[128 + y, b * 128 + n] += v
                else:
                    w[(256 + y) if y < 0 else y, b * 128 + n] += v
    return w


def lanes():
    return lax.broadcasted_iota(jnp.int32, (8, 128), 1)


def cat(a, b):
    return jnp.concatenate([a, b], 0)


def place(t, xg):
    return 4 * ((t % 4) * 8 + xg)


def pack_edges(old, t, xg, first, last):
    m = place(t, xg)
    lane = lanes()
    mixed = pltpu.roll(jnp.where(lane < 64, first, last), (m + 2) % 128, 1)
    return jnp.where((lane >> 2) == m // 4, mixed, old)


def merge_edges(left, right):
    return jnp.where((lanes() & 3) < 2, left, right)


def left_faces(left, own, flow):
    y = merge_edges(left, own)
    y1, y2, y3 = pltpu.roll(y, 1, 1), pltpu.roll(y, 2, 1), pltpu.roll(y, 3, 1)
    return flow * jnp.where(flow > 0, 5.0 * y2 + (2.0 * y1 - y3), 2.0 * y2 + (5.0 * y1 - y))


def advance(q, cf, sub, w, edges, faces, put, count, packed):
    lane16 = lax.broadcasted_iota(jnp.int32, (16, 128), 1)
    lane = lanes()
    half16 = lane16 < 64
    edge16 = (lane16 < 2) | (lane16 >= 126)
    main, second = [], []
    for xg in range(8):
        for t in range(0, count, 2):
            ts = [t, min(t + 1, count - 1)]
            av = [cat(*[q(u, j, 8 * xg) for u in ts]) for j in range(J)]
            uv = cat(*[pltpu.roll(edges[u // 4], (254 - place(u, xg)) % 128, 1) for u in ts]).astype(bf16)
            high = [a.astype(bf16) for a in av]
            for j in range(J):
                left = uv if j == 0 else high[j - 1]
                right = uv if j == J - 1 else high[j + 1]
                low = (av[j] - high[j].astype(f32)).astype(bf16)
                main.append(high[j])
                second.append(jnp.where(edge16, jnp.where(half16, right, left), low))
    lhs = jnp.concatenate([jnp.concatenate(main, 0), jnp.concatenate(second, 0)], 1)
    both = jnp.dot(lhs, w, preferred_element_type=f32)
    row = 0
    for xg in range(8):
        for t in range(0, count, 2):
            for u in range(2):
                if t + u >= count:
                    continue
                flux, moved = [], []
                for j in range(J):
                    r = slice((row + j) * 16 + u * 8, (row + j) * 16 + u * 8 + 8)
                    f = cf[j, xg, 4]
                    flux.append(f * jnp.where(f > 0, both[r, :128], both[r, 128:]))
                    moved.append(pltpu.roll(flux[j], 1, 1))
                before = pltpu.roll(faces[(t + u) // 4], (253 - place(t + u, xg)) % 128, 1)
                new = []
                for j in range(J):
                    x = [q(t + u, j, 8 * xg + d) for d in (-2, -1, 0, 1, 2)]
                    c = [cf[j, xg, k] for k in range(4)]
                    s = (c[0] * x[0] + c[1] * x[1]) + (c[2] * x[3] + c[3] * x[4])
                    v = cf[j, xg, 5 + 2 * sub] * x[2] - flux[j]
                    v = v + jnp.where(lane == 0, before if j == 0 else moved[j - 1], moved[j])
                    new.append((s + v) * cf[j, xg, 6 + 2 * sub])
                    put(t + u, j, xg, new[j])
                if packed is not None:
                    k = (t + u) // 4
                    packed[k] = pack_edges(packed[k], t + u, xg, new[0], new[J - 1])
            row += J
    return packed


def total(items):
    out = items[0]
    for item in items[1:]:
        out = out + item
    return out


def flag(condition):
    return jnp.where(condition, 1, 0).astype(jnp.int32)


def water_places(water_ref):
    ids = [water_ref[w] for w in range(NW)]
    halves = [i // NT for i in ids]
    ranks = [total([jnp.int32(0)] + [flag(halves[v] == halves[w]) for v in range(w)]) for w in range(NW)]
    ranks = [jnp.minimum(r, PW - 1) for r in ranks]
    return ids, halves, ranks


def first_kernel(
    slot_ref, water_ref, mass_ref, flux_ref, w_ref, tracers,
    q1, cf, lo2, hi2, zl2, zr2, z1, gpk, arrived,
    q0, q1v, up1, dn1, lo1, hi1, z0, zl1, zr1, up2, dn2, tsend, trecv, xsend, xrecv,
    mass, fx, fy, qw, qw1, upw, dnw, low, hiw, zw, zlw, zrw, q2w, wsend,
    load_sem, tile_ssem, tile_rsem, row_ssem, row_rsem, halo_ssem, halo_rsem,
    next_ssem, next_rsem, wh_ssem, wh_rsem, ws_sem, wr_sem, out_sem,
):
    grp, gx, gy = lax.axis_index("grp"), lax.axis_index("gx"), lax.axis_index("gy")
    me = (grp * NX + gx) * NY + gy
    pos = grp * NY + gy
    lane = lanes()

    def at(x, p):
        return {"grp": p // NY, "gx": x, "gy": lax.rem(p, NY)}

    def peer(k):
        return lax.rem(pos + k, GROUP)

    def load(c, j):
        return pltpu.make_async_copy(
            tracers.at[pl.ds(c * T, T), :, pl.ds(128 * j, 128)],
            q0.at[pl.ds(c * T, T), j, pl.ds(8, 64), :],
            load_sem.at[c, j],
        )

    def start_load(c, _):
        for j in range(J):
            load(c, j).start()
        return 0

    lax.fori_loop(0, CH, start_load, 0)

    barrier = pltpu.get_barrier_semaphore()

    def greet(device):
        pl.semaphore_signal(barrier, inc=1, device_id=device, device_id_type=MESH)

    for k in range(1, GROUP):
        greet(at(gx, peer(k)))

    @pl.when(gx > 0)
    def _():
        for k in range(GROUP):
            greet(at(gx - 1, peer(k)))

    @pl.when(gx < NX - 1)
    def _():
        for k in range(GROUP):
            greet(at(gx + 1, peer(k)))

    def held(c, only=None):
        choice = jnp.int32(0)
        for i in range(TPB) if only is None else (only,):
            g = slot_ref[(gx * NY + c) * TPB + i]
            choice = jnp.where(g // SLOTS == me, g % SLOTS, choice)
        return choice

    for c in range(NY):
        s = held(c)
        for j in range(J):
            cols = slice(128 * j, 128 * j + 128)
            tsend[c, pl.ds(16 * j, 16), :] = mass_ref[s, :, cols]
            tsend[c, pl.ds(48 + 16 * j, 16), :] = flux_ref[s, 0, :, cols]
            tsend[c, pl.ds(96 + 16 * j, 16), :] = flux_ref[s, 1, :, cols]
        if c > 0:
            b = held(c - 1)
            above = pltpu.roll(flux_ref[b, 1, pl.ds(8, 8), 256:384], 64, 1)
            tsend[c, pl.ds(144, 8), :] = jnp.where(lane < 64, above, flux_ref[b, 1, pl.ds(0, 8), 256:384])
        else:
            tsend[c, pl.ds(144, 8), :] = jnp.zeros((8, 128), f32)
        d = held(c, TPB - 1)
        xsend[c] = jnp.zeros((8, 128), f32)
        for j in range(J):
            xsend[c, pl.ds(j, 1), :] = flux_ref[d, 0, pl.ds(ROWS - 1, 1), 128 * j : 128 * j + 128]
    trecv[0] = tsend[gy]

    pl.semaphore_wait(barrier, GROUP - 1 + jnp.where(gx > 0, GROUP, 0) + jnp.where(gx < NX - 1, GROUP, 0))

    def tile_copy(k):
        return pltpu.make_async_remote_copy(
            src_ref=tsend.at[lax.rem(peer(k), NY)],
            dst_ref=trecv.at[k],
            send_sem=tile_ssem.at[k],
            recv_sem=tile_rsem.at[k],
            device_id=at(gx, peer(k)),
            device_id_type=MESH,
        )

    def row_copy(k):
        return pltpu.make_async_remote_copy(
            src_ref=xsend.at[lax.rem(peer(k), NY)],
            dst_ref=xrecv.at[k],
            send_sem=row_ssem.at[k],
            recv_sem=row_rsem.at[k],
            device_id=at(gx + 1, peer(k)),
            device_id_type=MESH,
        )

    for k in range(1, GROUP):
        tile_copy(k).start()

    @pl.when(gx < NX - 1)
    def _():
        for k in range(GROUP):
            row_copy(k).start()

    has = (gx < NX - 1, gx > 0, gy < NY - 1, gy > 0)
    get = (gx > 0, gx < NX - 1, gy > 0, gy < NY - 1)
    to = ({"gx": gx + 1}, {"gx": gx - 1}, {"gy": gy + 1}, {"gy": gy - 1})
    to = tuple({"grp": grp, "gx": gx, "gy": gy, **d} for d in to)

    def halo(d, src, dst, ssem, rsem):
        return pltpu.make_async_remote_copy(
            src_ref=src, dst_ref=dst, send_sem=ssem.at[d], recv_sem=rsem.at[d], device_id=to[d], device_id_type=MESH
        )

    sets1 = ((dn1, lo1), (up1, hi1), (z0, zl1), (z0, zr1))
    sets2 = ((dn2, lo2), (up2, hi2), (z1, zl2), (z1, zr2))
    setsw = ((dnw, low), (upw, hiw), (zw, zlw), (zw, zrw))

    def send_chunk(sets, c, ssem, rsem):
        for d, (src, dst) in enumerate(sets):

            @pl.when(has[d])
            def _(d=d, src=src, dst=dst):
                halo(d, src.at[c], dst.at[c], ssem, rsem).start()

    def wait_sets(sets, ssem, rsem, receive):
        for d, (src, dst) in enumerate(sets):
            copy = halo(d, src, dst, ssem, rsem)

            @pl.when(get[d] if receive else has[d])
            def _(copy=copy):
                (copy.wait_recv if receive else copy.wait_send)()

    def edge_rows(row):
        return [(t, j, (t * J + j) * 2) for t in range(row) for j in range(J)]

    def prepare(c, source, count):
        packed = [jnp.zeros((8, 128), f32)] * 2
        for t in range(count):
            for xg in range(8):
                packed[t // 4] = pack_edges(packed[t // 4], t, xg, source(t, 0, 8 * xg, 8), source(t, J - 1, 8 * xg, 8))
        for k in range(2):
            z0[c, k] = packed[k]
        for t, j, r in edge_rows(count):
            up1[c, pl.ds(r, 2), :] = source(t, j, 0, 2)
            dn1[c, pl.ds(r, 2), :] = source(t, j, 62, 2)
        send_chunk(sets1, c, halo_ssem, halo_rsem)

    def prepare_chunk(c, _):
        for j in range(J):
            load(c, j).wait()
        prepare(c, lambda t, j, r, n: q0[c * T + t, j, pl.ds(8 + r, n), :], T)
        return 0

    lax.fori_loop(0, CH, prepare_chunk, 0)

    ids, halves, ranks = water_places(water_ref)
    for p in range(PW):
        tracer = jnp.int32(0)
        for w in range(NW):
            tracer = jnp.where((halves[w] == grp) & (ranks[w] == p), ids[w] % NT, tracer)
        for j in range(J):
            qw[p, j, pl.ds(8, 64), :] = q0[tracer, j, pl.ds(8, 64), :]
    prepare(CH, lambda t, j, r, n: qw[t, j, pl.ds(8 + r, n), :], PW)

    for k in range(1, GROUP):
        tile_copy(k).wait_recv()

    @pl.when(gx > 0)
    def _():
        for k in range(GROUP):
            row_copy(k).wait_recv()

    def sender(tile):
        owner = slot_ref[tile] // SLOTS
        return lax.rem(pos + GROUP - (owner // (NX * NY) * NY + owner % NY), GROUP)

    base = (gx * NY + gy) * TPB
    left = []
    for i in range(TPB):
        k = sender(base + i)
        for j in range(J):
            mass[j, pl.ds(16 * i, 16), :] = trecv[k, pl.ds(16 * j, 16), :]
            fx[j, pl.ds(8 + 16 * i, 16), :] = trecv[k, pl.ds(48 + 16 * j, 16), :] * (1.0 / 12.0)
            fy[j, pl.ds(16 * i, 16), :] = trecv[k, pl.ds(96 + 16 * j, 16), :] * (1.0 / 12.0)
        k = sender(jnp.maximum(base - TPB, 0) + i)
        v = jnp.where(gy > 0, trecv[k, pl.ds(144, 8), :] * (1.0 / 12.0), 0.0)
        left += [v, pltpu.roll(v, 64, 1)]
    k = sender(jnp.maximum(base - NY * TPB, 0) + TPB - 1)
    for j in range(J):
        v = jnp.where(gx > 0, xrecv[k, pl.ds(j, 1), :] * (1.0 / 12.0), 0.0)
        fx[j, pl.ds(7, 1), :] = v
    g = jnp.zeros((8, 128), f32)
    for xg in range(8):
        g = jnp.where(lane == 4 * xg + 3, pltpu.roll(left[xg], 4 * xg + 4, 1), g)
    gpk[...] = (g + pltpu.roll(g, 32, 1)) + (pltpu.roll(g, 64, 1) + pltpu.roll(g, 96, 1))
    for xg in range(8):
        moved = []
        for j in range(J):
            f = fx[j, pl.ds(8 + 8 * xg, 8), :]
            b = fx[j, pl.ds(7 + 8 * xg, 8), :]
            fp, fm, gp, gm = jnp.maximum(f, 0.0), jnp.minimum(f, 0.0), jnp.maximum(b, 0.0), jnp.minimum(b, 0.0)
            h = fy[j, pl.ds(8 * xg, 8), :]
            moved.append(pltpu.roll(h, 1, 1))
            last = pltpu.roll(left[xg], 1, 1) if j == 0 else moved[j - 1]
            out = 6.0 * ((f - b) + (h - jnp.where(lane == 0, last, moved[j])))
            m0 = mass[j, pl.ds(8 * xg, 8), :]
            m1 = m0 - out
            m2 = m1 - out
            centre = (5.0 * fp + 2.0 * fm) - (2.0 * gp + 5.0 * gm)
            cf[j, xg, 0] = -gp
            cf[j, xg, 1] = fp + (5.0 * gp + 2.0 * gm)
            cf[j, xg, 2] = -(2.0 * fp + 5.0 * fm) - gm
            cf[j, xg, 3] = fm
            cf[j, xg, 4] = h
            cf[j, xg, 5] = m0 - centre
            cf[j, xg, 6] = 1.0 / m1
            cf[j, xg, 7] = m1 - centre
            cf[j, xg, 8] = 1.0 / m2

    wait_sets(sets1, halo_ssem, halo_rsem, True)

    def fill(dst, c, count, lo, hi):
        for t, j, r in edge_rows(count):
            dst(t, j, 6, jnp.where(get[0], lo[c, pl.ds(r, 2), :], 0.0))
            dst(t, j, 72, jnp.where(get[1], hi[c, pl.ds(r, 2), :], 0.0))

    def edge_terms(zl, zr, zo, c):
        zls = [jnp.where(get[2], zl[c, k], 0.0) for k in range(2)]
        zrs = [jnp.where(get[3], zr[c, k], 0.0) for k in range(2)]
        return [merge_edges(a, b) for a, b in zip(zls, zrs)], [left_faces(zls[k], zo[c, k], gpk[...]) for k in range(2)]

    def put_qw(t, j, r, v):
        qw[t, j, pl.ds(r, 2), :] = v

    fill(put_qw, CH, PW, lo1, hi1)
    edges, faces = edge_terms(zl1, zr1, z0, CH)

    def put_qw1(t, j, xg, v):
        qw1[t, j, pl.ds(8 + 8 * xg, 8), :] = v

    packed = advance(
        lambda t, j, r: qw[t, j, pl.ds(8 + r, 8), :], cf, 0, w_ref[...], edges, faces, put_qw1, PW,
        [jnp.zeros((8, 128), f32)] * 2,
    )
    for k in range(2):
        zw[0, k] = packed[k]
    for t, j, r in edge_rows(PW):
        upw[0, pl.ds(r, 2), :] = qw1[t, j, pl.ds(8, 2), :]
        dnw[0, pl.ds(r, 2), :] = qw1[t, j, pl.ds(70, 2), :]
    send_chunk(setsw, 0, wh_ssem, wh_rsem)

    def water_copy(k):
        return pltpu.make_async_remote_copy(
            src_ref=wsend.at[k],
            dst_ref=arrived.at[k],
            send_sem=ws_sem.at[k],
            recv_sem=wr_sem.at[k],
            device_id=at(gx, peer(k)),
            device_id_type=MESH,
        )

    def own_water():
        return pltpu.make_async_copy(wsend.at[0], arrived.at[0], ws_sem.at[0])

    def finish_water():
        wait_sets(setsw, wh_ssem, wh_rsem, True)

        def put_halo(t, j, r, v):
            qw1[t, j, pl.ds(r, 2), :] = v

        fill(put_halo, 0, PW, low, hiw)
        edges, faces = edge_terms(zlw, zrw, zw, 0)

        def put_q2(t, j, xg, v):
            q2w[xg // 2, t, j, pl.ds(8 * (xg % 2), 8), :] = v

        advance(
            lambda t, j, r: qw1[t, j, pl.ds(8 + r, 8), :], cf, 1, w_ref[...], edges, faces, put_q2, PW, None
        )
        for k in range(GROUP):
            p = peer(k)
            owners = [slot_ref[base + i] // SLOTS for i in range(TPB)]
            tile = jnp.int32(0)
            for i in range(TPB):
                tile = jnp.where(owners[i] // (NX * NY) * NY + owners[i] % NY == p, i, tile)
            wsend[k] = q2w[tile]
        own_water().start()
        for k in range(1, GROUP):
            water_copy(k).start()

    def out_copy(c):
        return pltpu.make_async_copy(q1v.at[pl.ds(c * T, T)], q1.at[pl.ds(c * T, T)], out_sem.at[0])

    def chunk(c, _):
        def put_q0(t, j, r, v):
            q0[c * T + t, j, pl.ds(r, 2), :] = v

        fill(put_q0, c, T, lo1, hi1)
        edges, faces = edge_terms(zl1, zr1, z0, c)

        def put_q1(t, j, xg, v):
            q1v[c * T + t, j, pl.ds(8 * xg, 8), :] = v

        packed = advance(
            lambda t, j, r: q0[c * T + t, j, pl.ds(8 + r, 8), :], cf, 0, w_ref[...], edges, faces, put_q1, T,
            [jnp.zeros((8, 128), f32)] * 2,
        )
        for k in range(2):
            z1[c, k] = packed[k]
        for t, j, r in edge_rows(T):
            up2[c, pl.ds(r, 2), :] = q1v[c * T + t, j, pl.ds(0, 2), :]
            dn2[c, pl.ds(r, 2), :] = q1v[c * T + t, j, pl.ds(62, 2), :]
        out_copy(c).start()
        send_chunk(sets2, c, next_ssem, next_rsem)

        @pl.when(c == 2)
        def _():
            finish_water()

        return 0

    lax.fori_loop(0, CH, chunk, 0)

    for k in range(1, GROUP):
        tile_copy(k).wait_send()

    @pl.when(gx < NX - 1)
    def _():
        for k in range(GROUP):
            row_copy(k).wait_send()

    wait_sets(sets1, halo_ssem, halo_rsem, False)
    wait_sets(setsw, wh_ssem, wh_rsem, False)
    wait_sets(sets2, next_ssem, next_rsem, False)
    wait_sets(sets2, next_ssem, next_rsem, True)
    pltpu.make_async_copy(q1v, q1, out_sem.at[0]).wait()
    own_water().wait()
    for k in range(1, GROUP):
        water_copy(k).wait()


def second_kernel(
    slot_ref, water_ref, w_ref, cf, lo, hi, zl, zr, zo, gpk, arrived, q1,
    out, water, qb, ob, in_sem, out_sem,
):
    grp, gx, gy = lax.axis_index("grp"), lax.axis_index("gx"), lax.axis_index("gy")
    me = (grp * NX + gx) * NY + gy
    pos = grp * NY + gy

    def load(c, s):
        return pltpu.make_async_copy(q1.at[pl.ds(c * T, T)], qb.at[s, :, :, pl.ds(8, 64), :], in_sem.at[s])

    def store(c, s, j):
        return pltpu.make_async_copy(
            ob.at[s, :, j], out.at[pl.ds(c * T, T), :, pl.ds(128 * j, 128)], out_sem.at[s, j]
        )

    load(0, 0).start()

    ids, halves, ranks = water_places(water_ref)
    for s in range(SLOTS):
        column, valid = jnp.int32(0), jnp.int32(0)
        for c in range(NY):
            for i in range(TPB):
                match = slot_ref[(gx * NY + c) * TPB + i] == me * SLOTS + s
                column = jnp.where(match, c, column)
                valid = jnp.where(match, 1, valid)
        for w in range(NW):
            k = lax.rem(pos + GROUP - (halves[w] * NY + column), GROUP)
            for j in range(J):
                water[s, w, :, 128 * j : 128 * j + 128] = jnp.where(valid > 0, arrived[k, ranks[w], j], 0.0)

    def chunk(c, _):
        s = lax.rem(c, 2)

        @pl.when(c + 1 < CH)
        def _():
            load(c + 1, 1 - s).start()

        load(c, s).wait()

        @pl.when(c >= 2)
        def _():
            for j in range(J):
                store(c - 2, s, j).wait()

        for t in range(T):
            for j in range(J):
                r = (t * J + j) * 2
                qb[s, t, j, pl.ds(6, 2), :] = jnp.where(gx > 0, lo[c, pl.ds(r, 2), :], 0.0)
                qb[s, t, j, pl.ds(72, 2), :] = jnp.where(gx < NX - 1, hi[c, pl.ds(r, 2), :], 0.0)
        zls = [jnp.where(gy > 0, zl[c, k], 0.0) for k in range(2)]
        zrs = [jnp.where(gy < NY - 1, zr[c, k], 0.0) for k in range(2)]
        edges = [merge_edges(a, b) for a, b in zip(zls, zrs)]
        faces = [left_faces(zls[k], zo[c, k], gpk[...]) for k in range(2)]

        def put(t, j, xg, v):
            ob[s, t, j, pl.ds(8 * xg, 8), :] = v

        advance(lambda t, j, r: qb[s, t, j, pl.ds(8 + r, 8), :], cf, 1, w_ref[...], edges, faces, put, T, None)
        for j in range(J):
            store(c, s, j).start()
        return 0

    lax.fori_loop(0, CH, chunk, 0)
    for c in (CH - 2, CH - 1):
        for j in range(J):
            store(c, c % 2, j).wait()


def per_device(tracers, dycore_air_mass, dycore_face_flux, tile_dycore_slot, water_idx):
    weights = jnp.asarray(stencil_weights(), bf16)
    smem = pl.BlockSpec(memory_space=pltpu.SMEM)
    vmem = pl.BlockSpec(memory_space=pltpu.VMEM)
    hbm = pl.BlockSpec(memory_space=pl.ANY)
    V, D = pltpu.VMEM, pltpu.SemaphoreType.DMA

    def S(*shape):
        return jax.ShapeDtypeStruct(shape, f32)

    edge, packs = (EDGE, 128), (2, 8, 128)
    scratch = [
        V((NT, J, 80, 128), f32), V((NT, J, 64, 128), f32),
        V((CH + 1, *edge), f32), V((CH + 1, *edge), f32), V((CH + 1, *edge), f32), V((CH + 1, *edge), f32),
        V((CH + 1, *packs), f32), V((CH + 1, *packs), f32), V((CH + 1, *packs), f32),
        V((CH, *edge), f32), V((CH, *edge), f32),
        V((NY, 152, 128), f32), V((GROUP, 152, 128), f32), V((NY, 8, 128), f32), V((GROUP, 8, 128), f32),
        V((J, 64, 128), f32), V((J, 72, 128), f32), V((J, 64, 128), f32),
        V((PW, J, 80, 128), f32), V((PW, J, 80, 128), f32),
        V((1, *edge), f32), V((1, *edge), f32), V((1, *edge), f32), V((1, *edge), f32),
        V((1, *packs), f32), V((1, *packs), f32), V((1, *packs), f32),
        V((TPB, PW, J, ROWS, 128), f32), V((GROUP, PW, J, ROWS, 128), f32),
        D((CH, J)), D((GROUP,)), D((GROUP,)), D((GROUP,)), D((GROUP,)), D((4,)), D((4,)),
        D((4,)), D((4,)), D((4,)), D((4,)), D((GROUP,)), D((GROUP,)), D((1,)),
    ]
    q1, cf, lo, hi, zl, zr, zo, gpk, arrived = pl.pallas_call(
        first_kernel,
        out_shape=(
            S(NT, J, 64, 128), S(J, 8, 9, 8, 128), S(CH, *edge), S(CH, *edge), S(CH, *packs), S(CH, *packs),
            S(CH, *packs), S(8, 128), S(GROUP, PW, J, ROWS, 128),
        ),
        in_specs=[smem, smem, vmem, vmem, vmem, hbm],
        out_specs=(hbm, vmem, hbm, hbm, hbm, hbm, vmem, vmem, hbm),
        scratch_shapes=scratch,
        compiler_params=pltpu.CompilerParams(
            collective_id=0, has_side_effects=True, vmem_limit_bytes=60 * 2**20
        ),
        name="first_substep",
    )(tile_dycore_slot, water_idx, dycore_air_mass, dycore_face_flux, weights, tracers)
    return pl.pallas_call(
        second_kernel,
        out_shape=(S(NT, 64, J * 128), S(SLOTS, NW, ROWS, J * 128)),
        in_specs=[smem, smem] + [vmem] * 9 + [hbm],
        out_specs=(hbm, vmem),
        scratch_shapes=[V((2, T, J, 80, 128), f32), V((2, T, J, 64, 128), f32), D((2,)), D((2, J))],
        compiler_params=pltpu.CompilerParams(vmem_limit_bytes=60 * 2**20),
        name="second_substep",
    )(tile_dycore_slot, water_idx, weights, cf, lo, hi, zl, zr, zo, gpk, arrived, q1)


def solution(mesh):
    return jax.shard_map(
        per_device,
        mesh=mesh,
        in_specs=(
            P("grp", "gx", "gy"),
            P(("grp", "gx", "gy"), None, None),
            P(("grp", "gx", "gy"), None, None, None),
            P(),
            P(),
        ),
        out_specs=(P("grp", "gx", "gy"), P(("grp", "gx", "gy"), None, None, None)),
        check_vma=False,
    )
```

```python
import jax
import jax.numpy as jnp
import numpy as np
from jax import lax
from jax.experimental import pallas as pl
from jax.experimental.pallas import tpu as pltpu
from jax.sharding import PartitionSpec as P

MESH = pl.DeviceIdType.MESH
f32 = jnp.float32
bf16 = jnp.bfloat16

NG, NX, NY = 2, 16, 4
GROUP = NG * NY
TPB = 4
SLOTS = 4
ROWS = 16
J = 3
T = 8
NT = 128
CH = NT // T
NW = 6
PW = 5
EDGE = T * J * 2
SET = T // 2 * J


def stencil_weights():
    w = np.zeros((256, 512), np.float32)
    for b, (shift, taps) in enumerate(
        (s, t) for s in (0, -1) for t in ({-1: -1, 0: 5, 1: 2}, {0: 2, 1: 5, 2: -1})
    ):
        for n in range(128):
            for d, v in taps.items():
                y = n + d + shift
                if 0 <= y < 128:
                    w[y, b * 128 + n] += v
                    if 2 <= y < 126:
                        w[128 + y, b * 128 + n] += v
                else:
                    w[(256 + y) if y < 0 else y, b * 128 + n] += v
    return w


def lanes():
    return lax.broadcasted_iota(jnp.int32, (8, 128), 1)


def cat(a, b):
    return jnp.concatenate([a, b], 0)


def place(t, xg):
    return 4 * ((t % 4) * 8 + xg)


def pack_edges(old, t, xg, first, last):
    m = place(t, xg)
    lane = lanes()
    mixed = pltpu.roll(jnp.where(lane < 64, first, last), (m + 2) % 128, 1)
    return jnp.where((lane >> 2) == m // 4, mixed, old)


def merge_edges(left, right):
    return jnp.where((lanes() & 3) < 2, left, right)


def load_weights(w_ref, accs):
    for m in range(2):
        pltpu.matmul_push_rhs(w_ref[:, 256 * m : 256 * m + 256], 0, m)
        pltpu.matmul_acc_lhs(accs[m][0], jnp.zeros((16, 256), bf16), load_staged_rhs=0)
        pltpu.matmul_pop(accs[m][0])


def issue_row(q, accs, base, edges, count, xg):
    lane16 = lax.broadcasted_iota(jnp.int32, (16, 128), 1)
    half16 = lane16 < 64
    edge16 = (lane16 < 2) | (lane16 >= 126)
    for t in range(0, count, 2):
        ts = [t, min(t + 1, count - 1)]
        both = [cat(*[q(u, j, 8 * xg) for u in ts]) for j in range(J)]
        outer = cat(*[pltpu.roll(edges[u // 4], (254 - place(u, xg)) % 128, 1) for u in ts]).astype(bf16)
        high = [a.astype(bf16) for a in both]
        for j in range(J):
            left = outer if j == 0 else high[j - 1]
            right = outer if j == J - 1 else high[j + 1]
            low = (both[j] - high[j].astype(f32)).astype(bf16)
            second = jnp.where(edge16, jnp.where(half16, right, left), low)
            lhs = jnp.concatenate([high[j], second], 1)
            for m in range(2):
                pltpu.matmul_acc_lhs(accs[m][base], lhs)
            base += 1


def finish_row(q, cf, sub, accs, base, put, count, xg, packed):
    for t in range(0, count, 2):
        new = {}
        for j in range(J):
            c = [cf[j, xg, 7 * sub + k] for k in range(7)]
            upper, lower = (pltpu.matmul_pop(accs[m][base]) for m in range(2))
            base += 1
            for u in range(min(2, count - t)):
                r = slice(8 * u, 8 * u + 8)
                x = [q(t + u, j, 8 * xg + d) for d in (-2, -1, 0, 1, 2)]
                s = (c[0] * x[0] + c[1] * x[1]) + (c[2] * x[2] + c[3] * x[3])
                v = c[4] * x[4] + c[5] * jnp.where(c[5] < 0, upper[r, :128], upper[r, 128:])
                v = v + c[6] * jnp.where(c[6] > 0, lower[r, :128], lower[r, 128:])
                new[u, j] = s + v
                put(t + u, j, xg, new[u, j])
        if packed is not None:
            for u in range(min(2, count - t)):
                k = (t + u) // 4
                packed[k] = pack_edges(packed[k], t + u, xg, new[u, 0], new[u, J - 1])


def advance(q, cf, sub, accs, edges, put, count, packed):
    issue_row(q, accs, 0, edges, count, 0)
    for xg in range(8):
        if xg < 7:
            issue_row(q, accs, (xg + 1) % 2 * SET, edges, count, xg + 1)
        finish_row(q, cf, sub, accs, xg % 2 * SET, put, count, xg, packed)
    return packed


def with_accumulators(body):
    n = 2 * SET
    pl.run_scoped(lambda *a: body((a[:n], a[n:])), *[pltpu.ACC(i // n)((16, 256), f32) for i in range(2 * n)])


def total(items):
    out = items[0]
    for item in items[1:]:
        out = out + item
    return out


def flag(condition):
    return jnp.where(condition, 1, 0).astype(jnp.int32)


def water_places(water_ref):
    ids = [water_ref[w] for w in range(NW)]
    halves = [i // NT for i in ids]
    ranks = [total([jnp.int32(0)] + [flag(halves[v] == halves[w]) for v in range(w)]) for w in range(NW)]
    ranks = [jnp.minimum(r, PW - 1) for r in ranks]
    return ids, halves, ranks


def first_kernel(*refs):
    with_accumulators(lambda accs: first_body(accs, *refs))


def first_body(
    accs,
    slot_ref, water_ref, mass_ref, flux_ref, w_ref, tracers,
    q1, cf, lo2, hi2, zl2, zr2, arrived,
    q0, q1v, z1, up1, dn1, lo1, hi1, z0, zl1, zr1, up2, dn2, tsend, trecv, xsend, xrecv,
    mass, fx, fy, qw, qw1, upw, dnw, low, hiw, zw, zlw, zrw, q2w, wsend,
    load_sem, tile_ssem, tile_rsem, row_ssem, row_rsem, halo_ssem, halo_rsem,
    next_ssem, next_rsem, wh_ssem, wh_rsem, ws_sem, wr_sem, out_sem,
):
    grp, gx, gy = lax.axis_index("grp"), lax.axis_index("gx"), lax.axis_index("gy")
    me = (grp * NX + gx) * NY + gy
    pos = grp * NY + gy
    lane = lanes()

    def at(x, p):
        return {"grp": p // NY, "gx": x, "gy": lax.rem(p, NY)}

    def peer(k):
        return lax.rem(pos + k, GROUP)

    def load(c, j):
        return pltpu.make_async_copy(
            tracers.at[pl.ds(c * T, T), :, pl.ds(128 * j, 128)],
            q0.at[pl.ds(c * T, T), j, pl.ds(8, 64), :],
            load_sem.at[c, j],
        )

    def start_load(c, _):
        for j in range(J):
            load(c, j).start()
        return 0

    lax.fori_loop(0, CH, start_load, 0)
    load_weights(w_ref, accs)

    barrier = pltpu.get_barrier_semaphore()

    def greet(device):
        pl.semaphore_signal(barrier, inc=1, device_id=device, device_id_type=MESH)

    for k in range(1, GROUP):
        greet(at(gx, peer(k)))

    @pl.when(gx > 0)
    def _():
        for k in range(GROUP):
            greet(at(gx - 1, peer(k)))

    @pl.when(gx < NX - 1)
    def _():
        for k in range(GROUP):
            greet(at(gx + 1, peer(k)))

    def held(c, only=None):
        choice = jnp.int32(0)
        for i in range(TPB) if only is None else (only,):
            g = slot_ref[(gx * NY + c) * TPB + i]
            choice = jnp.where(g // SLOTS == me, g % SLOTS, choice)
        return choice

    for c in range(NY):
        s = held(c)
        for j in range(J):
            cols = slice(128 * j, 128 * j + 128)
            tsend[c, pl.ds(16 * j, 16), :] = mass_ref[s, :, cols]
            tsend[c, pl.ds(48 + 16 * j, 16), :] = flux_ref[s, 0, :, cols]
            tsend[c, pl.ds(96 + 16 * j, 16), :] = flux_ref[s, 1, :, cols]
        if c > 0:
            b = held(c - 1)
            above = pltpu.roll(flux_ref[b, 1, pl.ds(8, 8), 256:384], 64, 1)
            tsend[c, pl.ds(144, 8), :] = jnp.where(lane < 64, above, flux_ref[b, 1, pl.ds(0, 8), 256:384])
        else:
            tsend[c, pl.ds(144, 8), :] = jnp.zeros((8, 128), f32)
        d = held(c, TPB - 1)
        xsend[c] = jnp.zeros((8, 128), f32)
        for j in range(J):
            xsend[c, pl.ds(j, 1), :] = flux_ref[d, 0, pl.ds(ROWS - 1, 1), 128 * j : 128 * j + 128]
    trecv[0] = tsend[gy]

    pl.semaphore_wait(barrier, GROUP - 1 + jnp.where(gx > 0, GROUP, 0) + jnp.where(gx < NX - 1, GROUP, 0))

    def tile_copy(k):
        return pltpu.make_async_remote_copy(
            src_ref=tsend.at[lax.rem(peer(k), NY)],
            dst_ref=trecv.at[k],
            send_sem=tile_ssem.at[k],
            recv_sem=tile_rsem.at[k],
            device_id=at(gx, peer(k)),
            device_id_type=MESH,
        )

    def row_copy(k):
        return pltpu.make_async_remote_copy(
            src_ref=xsend.at[lax.rem(peer(k), NY)],
            dst_ref=xrecv.at[k],
            send_sem=row_ssem.at[k],
            recv_sem=row_rsem.at[k],
            device_id=at(gx + 1, peer(k)),
            device_id_type=MESH,
        )

    for k in range(1, GROUP):
        tile_copy(k).start()

    @pl.when(gx < NX - 1)
    def _():
        for k in range(GROUP):
            row_copy(k).start()

    has = (gx < NX - 1, gx > 0, gy < NY - 1, gy > 0)
    get = (gx > 0, gx < NX - 1, gy > 0, gy < NY - 1)
    to = ({"gx": gx + 1}, {"gx": gx - 1}, {"gy": gy + 1}, {"gy": gy - 1})
    to = tuple({"grp": grp, "gx": gx, "gy": gy, **d} for d in to)

    def halo(d, src, dst, ssem, rsem):
        return pltpu.make_async_remote_copy(
            src_ref=src, dst_ref=dst, send_sem=ssem.at[d], recv_sem=rsem.at[d], device_id=to[d], device_id_type=MESH
        )

    sets1 = ((dn1, lo1), (up1, hi1), (z0, zl1), (z0, zr1))
    sets2 = ((dn2, lo2), (up2, hi2), (z1, zl2), (z1, zr2))
    setsw = ((dnw, low), (upw, hiw), (zw, zlw), (zw, zrw))

    def send_chunk(sets, c, ssem, rsem):
        for d, (src, dst) in enumerate(sets):

            @pl.when(has[d])
            def _(d=d, src=src, dst=dst):
                halo(d, src.at[c], dst.at[c], ssem, rsem).start()

    def wait_sets(sets, ssem, rsem, receive):
        for d, (src, dst) in enumerate(sets):
            copy = halo(d, src, dst, ssem, rsem)

            @pl.when(get[d] if receive else has[d])
            def _(copy=copy):
                (copy.wait_recv if receive else copy.wait_send)()

    def edge_rows(row):
        return [(t, j, (t * J + j) * 2) for t in range(row) for j in range(J)]

    def prepare(c, source, count):
        packed = [jnp.zeros((8, 128), f32)] * 2
        for t in range(count):
            for xg in range(8):
                packed[t // 4] = pack_edges(packed[t // 4], t, xg, source(t, 0, 8 * xg, 8), source(t, J - 1, 8 * xg, 8))
        for k in range(2):
            z0[c, k] = packed[k]
        for t, j, r in edge_rows(count):
            up1[c, pl.ds(r, 2), :] = source(t, j, 0, 2)
            dn1[c, pl.ds(r, 2), :] = source(t, j, 62, 2)
        send_chunk(sets1, c, halo_ssem, halo_rsem)

    def prepare_chunk(c, _):
        for j in range(J):
            load(c, j).wait()
        prepare(c, lambda t, j, r, n: q0[c * T + t, j, pl.ds(8 + r, n), :], T)
        return 0

    lax.fori_loop(0, CH, prepare_chunk, 0)

    ids, halves, ranks = water_places(water_ref)
    for p in range(PW):
        tracer = jnp.int32(0)
        for w in range(NW):
            tracer = jnp.where((halves[w] == grp) & (ranks[w] == p), ids[w] % NT, tracer)
        for j in range(J):
            qw[p, j, pl.ds(8, 64), :] = q0[tracer, j, pl.ds(8, 64), :]
    prepare(CH, lambda t, j, r, n: qw[t, j, pl.ds(8 + r, n), :], PW)

    for k in range(1, GROUP):
        tile_copy(k).wait_recv()

    @pl.when(gx > 0)
    def _():
        for k in range(GROUP):
            row_copy(k).wait_recv()

    def sender(tile):
        owner = slot_ref[tile] // SLOTS
        return lax.rem(pos + GROUP - (owner // (NX * NY) * NY + owner % NY), GROUP)

    base = (gx * NY + gy) * TPB
    left = []
    for i in range(TPB):
        k = sender(base + i)
        for j in range(J):
            mass[j, pl.ds(16 * i, 16), :] = trecv[k, pl.ds(16 * j, 16), :]
            fx[j, pl.ds(8 + 16 * i, 16), :] = trecv[k, pl.ds(48 + 16 * j, 16), :] * (1.0 / 12.0)
            fy[j, pl.ds(16 * i, 16), :] = trecv[k, pl.ds(96 + 16 * j, 16), :] * (1.0 / 12.0)
        k = sender(jnp.maximum(base - TPB, 0) + i)
        v = jnp.where(gy > 0, trecv[k, pl.ds(144, 8), :] * (1.0 / 12.0), 0.0)
        left += [v, pltpu.roll(v, 64, 1)]
    k = sender(jnp.maximum(base - NY * TPB, 0) + TPB - 1)
    for j in range(J):
        v = jnp.where(gx > 0, xrecv[k, pl.ds(j, 1), :] * (1.0 / 12.0), 0.0)
        fx[j, pl.ds(7, 1), :] = v
    for xg in range(8):
        moved = []
        for j in range(J):
            f = fx[j, pl.ds(8 + 8 * xg, 8), :]
            b = fx[j, pl.ds(7 + 8 * xg, 8), :]
            fp, fm, gp, gm = jnp.maximum(f, 0.0), jnp.minimum(f, 0.0), jnp.maximum(b, 0.0), jnp.minimum(b, 0.0)
            h = fy[j, pl.ds(8 * xg, 8), :]
            moved.append(pltpu.roll(h, 1, 1))
            last = pltpu.roll(left[xg], 1, 1) if j == 0 else moved[j - 1]
            h0 = jnp.where(lane == 0, last, moved[j])
            out = 6.0 * ((f - b) + (h - h0))
            m0 = mass[j, pl.ds(8 * xg, 8), :]
            centre = (5.0 * fp + 2.0 * fm) - (2.0 * gp + 5.0 * gm)
            for sub in range(2):
                m1 = m0 - out
                inv = 1.0 / m1
                for k, v in enumerate(
                    (-gp, fp + (5.0 * gp + 2.0 * gm), m0 - centre, -(2.0 * fp + 5.0 * fm) - gm, fm, -h, h0)
                ):
                    cf[j, xg, 7 * sub + k] = v * inv
                m0 = m1

    wait_sets(sets1, halo_ssem, halo_rsem, True)

    def fill(dst, c, count, lo, hi):
        for t, j, r in edge_rows(count):
            dst(t, j, 6, jnp.where(get[0], lo[c, pl.ds(r, 2), :], 0.0))
            dst(t, j, 72, jnp.where(get[1], hi[c, pl.ds(r, 2), :], 0.0))

    def edge_terms(zl, zr, c):
        return [
            merge_edges(jnp.where(get[2], zl[c, k], 0.0), jnp.where(get[3], zr[c, k], 0.0)) for k in range(2)
        ]

    def put_qw(t, j, r, v):
        qw[t, j, pl.ds(r, 2), :] = v

    fill(put_qw, CH, PW, lo1, hi1)
    edges = edge_terms(zl1, zr1, CH)

    def put_qw1(t, j, xg, v):
        qw1[t, j, pl.ds(8 + 8 * xg, 8), :] = v

    packed = advance(
        lambda t, j, r: qw[t, j, pl.ds(8 + r, 8), :], cf, 0, accs, edges, put_qw1, PW,
        [jnp.zeros((8, 128), f32)] * 2,
    )
    for k in range(2):
        zw[0, k] = packed[k]
    for t, j, r in edge_rows(PW):
        upw[0, pl.ds(r, 2), :] = qw1[t, j, pl.ds(8, 2), :]
        dnw[0, pl.ds(r, 2), :] = qw1[t, j, pl.ds(70, 2), :]
    send_chunk(setsw, 0, wh_ssem, wh_rsem)

    def water_copy(k):
        return pltpu.make_async_remote_copy(
            src_ref=wsend.at[k],
            dst_ref=arrived.at[k],
            send_sem=ws_sem.at[k],
            recv_sem=wr_sem.at[k],
            device_id=at(gx, peer(k)),
            device_id_type=MESH,
        )

    def own_water():
        return pltpu.make_async_copy(wsend.at[0], arrived.at[0], ws_sem.at[0])

    def finish_water():
        wait_sets(setsw, wh_ssem, wh_rsem, True)

        def put_halo(t, j, r, v):
            qw1[t, j, pl.ds(r, 2), :] = v

        fill(put_halo, 0, PW, low, hiw)
        edges = edge_terms(zlw, zrw, 0)

        def put_q2(t, j, xg, v):
            q2w[xg // 2, t, j, pl.ds(8 * (xg % 2), 8), :] = v

        advance(
            lambda t, j, r: qw1[t, j, pl.ds(8 + r, 8), :], cf, 1, accs, edges, put_q2, PW, None
        )
        for k in range(GROUP):
            p = peer(k)
            owners = [slot_ref[base + i] // SLOTS for i in range(TPB)]
            tile = jnp.int32(0)
            for i in range(TPB):
                tile = jnp.where(owners[i] // (NX * NY) * NY + owners[i] % NY == p, i, tile)
            wsend[k] = q2w[tile]
        own_water().start()
        for k in range(1, GROUP):
            water_copy(k).start()

    def out_copy(c):
        return pltpu.make_async_copy(q1v.at[pl.ds(c * T, T)], q1.at[pl.ds(c * T, T)], out_sem.at[0])

    def chunk(c, _):
        def put_q0(t, j, r, v):
            q0[c * T + t, j, pl.ds(r, 2), :] = v

        fill(put_q0, c, T, lo1, hi1)
        edges = edge_terms(zl1, zr1, c)

        def put_q1(t, j, xg, v):
            q1v[c * T + t, j, pl.ds(8 * xg, 8), :] = v

        packed = advance(
            lambda t, j, r: q0[c * T + t, j, pl.ds(8 + r, 8), :], cf, 0, accs, edges, put_q1, T,
            [jnp.zeros((8, 128), f32)] * 2,
        )
        for k in range(2):
            z1[c, k] = packed[k]
        for t, j, r in edge_rows(T):
            up2[c, pl.ds(r, 2), :] = q1v[c * T + t, j, pl.ds(0, 2), :]
            dn2[c, pl.ds(r, 2), :] = q1v[c * T + t, j, pl.ds(62, 2), :]
        out_copy(c).start()
        send_chunk(sets2, c, next_ssem, next_rsem)

        @pl.when(c == 2)
        def _():
            finish_water()

        return 0

    lax.fori_loop(0, CH, chunk, 0)

    for k in range(1, GROUP):
        tile_copy(k).wait_send()

    @pl.when(gx < NX - 1)
    def _():
        for k in range(GROUP):
            row_copy(k).wait_send()

    wait_sets(sets1, halo_ssem, halo_rsem, False)
    wait_sets(setsw, wh_ssem, wh_rsem, False)
    wait_sets(sets2, next_ssem, next_rsem, False)
    wait_sets(sets2, next_ssem, next_rsem, True)
    pltpu.make_async_copy(q1v, q1, out_sem.at[0]).wait()
    own_water().wait()
    for k in range(1, GROUP):
        water_copy(k).wait()


def second_kernel(*refs):
    with_accumulators(lambda accs: second_body(accs, *refs))


def second_body(
    accs,
    slot_ref, water_ref, w_ref, cf, lo, hi, zl, zr, arrived, q1,
    out, water, qb, ob, in_sem, out_sem,
):
    grp, gx, gy = lax.axis_index("grp"), lax.axis_index("gx"), lax.axis_index("gy")
    me = (grp * NX + gx) * NY + gy
    pos = grp * NY + gy

    def load(c):
        return pltpu.make_async_copy(q1.at[pl.ds(c * T, T)], qb.at[pl.ds(c * T, T), :, pl.ds(8, 64), :], in_sem.at[c])

    def store(c):
        return pltpu.make_async_copy(ob.at[pl.ds(c * T, T)], out.at[pl.ds(c * T, T)], out_sem.at[c])

    def each(body):
        def step(c, _):
            body(c)
            return 0

        lax.fori_loop(0, CH, step, 0)

    each(lambda c: load(c).start())
    load_weights(w_ref, accs)

    ids, halves, ranks = water_places(water_ref)
    for s in range(SLOTS):
        column, valid = jnp.int32(0), jnp.int32(0)
        for c in range(NY):
            for i in range(TPB):
                match = slot_ref[(gx * NY + c) * TPB + i] == me * SLOTS + s
                column = jnp.where(match, c, column)
                valid = jnp.where(match, 1, valid)
        for w in range(NW):
            k = lax.rem(pos + GROUP - (halves[w] * NY + column), GROUP)
            for j in range(J):
                water[s, w, :, 128 * j : 128 * j + 128] = jnp.where(valid > 0, arrived[k, ranks[w], j], 0.0)

    def chunk(c):
        load(c).wait()
        for t in range(T):
            for j in range(J):
                r = (t * J + j) * 2
                qb[c * T + t, j, pl.ds(6, 2), :] = jnp.where(gx > 0, lo[c, pl.ds(r, 2), :], 0.0)
                qb[c * T + t, j, pl.ds(72, 2), :] = jnp.where(gx < NX - 1, hi[c, pl.ds(r, 2), :], 0.0)
        edges = [
            merge_edges(jnp.where(gy > 0, zl[c, k], 0.0), jnp.where(gy < NY - 1, zr[c, k], 0.0)) for k in range(2)
        ]

        def put(t, j, xg, v):
            ob[c * T + t, pl.ds(8 * xg, 8), 128 * j : 128 * j + 128] = v

        advance(lambda t, j, r: qb[c * T + t, j, pl.ds(8 + r, 8), :], cf, 1, accs, edges, put, T, None)
        store(c).start()

    each(chunk)
    each(lambda c: store(c).wait())


def per_device(tracers, dycore_air_mass, dycore_face_flux, tile_dycore_slot, water_idx):
    weights = jnp.asarray(stencil_weights(), bf16)
    smem = pl.BlockSpec(memory_space=pltpu.SMEM)
    vmem = pl.BlockSpec(memory_space=pltpu.VMEM)
    hbm = pl.BlockSpec(memory_space=pl.ANY)
    V, D = pltpu.VMEM, pltpu.SemaphoreType.DMA

    def S(*shape):
        return jax.ShapeDtypeStruct(shape, f32)

    edge, packs = (EDGE, 128), (2, 8, 128)
    scratch = [
        V((NT, J, 80, 128), f32), V((NT, J, 64, 128), f32), V((CH, *packs), f32),
        V((CH + 1, *edge), f32), V((CH + 1, *edge), f32), V((CH + 1, *edge), f32), V((CH + 1, *edge), f32),
        V((CH + 1, *packs), f32), V((CH + 1, *packs), f32), V((CH + 1, *packs), f32),
        V((CH, *edge), f32), V((CH, *edge), f32),
        V((NY, 152, 128), f32), V((GROUP, 152, 128), f32), V((NY, 8, 128), f32), V((GROUP, 8, 128), f32),
        V((J, 64, 128), f32), V((J, 72, 128), f32), V((J, 64, 128), f32),
        V((PW, J, 80, 128), f32), V((PW, J, 80, 128), f32),
        V((1, *edge), f32), V((1, *edge), f32), V((1, *edge), f32), V((1, *edge), f32),
        V((1, *packs), f32), V((1, *packs), f32), V((1, *packs), f32),
        V((TPB, PW, J, ROWS, 128), f32), V((GROUP, PW, J, ROWS, 128), f32),
        D((CH, J)), D((GROUP,)), D((GROUP,)), D((GROUP,)), D((GROUP,)), D((4,)), D((4,)),
        D((4,)), D((4,)), D((4,)), D((4,)), D((GROUP,)), D((GROUP,)), D((1,)),
    ]
    q1, cf, lo, hi, zl, zr, arrived = pl.pallas_call(
        first_kernel,
        out_shape=(
            S(NT, J, 64, 128), S(J, 8, 14, 8, 128), S(CH, *edge), S(CH, *edge), S(CH, *packs), S(CH, *packs),
            S(GROUP, PW, J, ROWS, 128),
        ),
        in_specs=[smem, smem, vmem, vmem, vmem, hbm],
        out_specs=(hbm, vmem, hbm, hbm, hbm, hbm, hbm),
        scratch_shapes=scratch,
        compiler_params=pltpu.CompilerParams(
            collective_id=0, has_side_effects=True, vmem_limit_bytes=60 * 2**20
        ),
        name="first_substep",
    )(tile_dycore_slot, water_idx, dycore_air_mass, dycore_face_flux, weights, tracers)
    return pl.pallas_call(
        second_kernel,
        out_shape=(S(NT, 64, J * 128), S(SLOTS, NW, ROWS, J * 128)),
        in_specs=[smem, smem] + [vmem] * 7 + [hbm],
        out_specs=(hbm, vmem),
        scratch_shapes=[V((NT, J, 80, 128), f32), V((NT, 64, J * 128), f32), D((CH,)), D((CH,))],
        compiler_params=pltpu.CompilerParams(vmem_limit_bytes=60 * 2**20),
        name="second_substep",
    )(tile_dycore_slot, water_idx, weights, cf, lo, hi, zl, zr, arrived, q1)


def solution(mesh):
    return jax.shard_map(
        per_device,
        mesh=mesh,
        in_specs=(
            P("grp", "gx", "gy"),
            P(("grp", "gx", "gy"), None, None),
            P(("grp", "gx", "gy"), None, None, None),
            P(),
            P(),
        ),
        out_specs=(P("grp", "gx", "gy"), P(("grp", "gx", "gy"), None, None, None)),
        check_vma=False,
    )
```

```python
import jax
import jax.numpy as jnp
import numpy as np
from jax import lax
from jax.experimental import pallas as pl
from jax.experimental.pallas import tpu as pltpu
from jax.sharding import PartitionSpec as P

MESH = pl.DeviceIdType.MESH
f32 = jnp.float32
bf16 = jnp.bfloat16

NG, NX, NY = 2, 16, 4
GROUP = NG * NY
TPB = 4
SLOTS = 4
ROWS = 16
J = 3
T = 8
NT = 128
CH = NT // T
NW = 6
PW = 5
EDGE = T * J * 2
SET = T // 2 * J


def stencil_weights():
    w = np.zeros((256, 512), np.float32)
    for b, (shift, taps) in enumerate(
        (s, t) for s in (0, -1) for t in ({-1: -1, 0: 5, 1: 2}, {0: 2, 1: 5, 2: -1})
    ):
        for n in range(128):
            for d, v in taps.items():
                y = n + d + shift
                if 0 <= y < 128:
                    w[y, b * 128 + n] += v
                    if 2 <= y < 126:
                        w[128 + y, b * 128 + n] += v
                else:
                    w[(256 + y) if y < 0 else y, b * 128 + n] += v
    return w


def lanes():
    return lax.broadcasted_iota(jnp.int32, (8, 128), 1)


def cat(a, b):
    return jnp.concatenate([a, b], 0)


def place(t, xg):
    return 4 * ((t % 4) * 8 + xg)


def pack_edges(old, t, xg, first, last):
    m = place(t, xg)
    lane = lanes()
    mixed = pltpu.roll(jnp.where(lane < 64, first, last), (m + 2) % 128, 1)
    return jnp.where((lane >> 2) == m // 4, mixed, old)


def merge_edges(left, right):
    return jnp.where((lanes() & 3) < 2, left, right)


def load_weights(w_ref, accs):
    for m in range(2):
        pltpu.matmul_push_rhs(w_ref[:, 256 * m : 256 * m + 256], 0, m)
        pltpu.matmul_acc_lhs(accs[m][0], jnp.zeros((16, 256), bf16), load_staged_rhs=0)
        pltpu.matmul_pop(accs[m][0])


def issue_row(q, accs, base, edges, count, xg):
    lane16 = lax.broadcasted_iota(jnp.int32, (16, 128), 1)
    half16 = lane16 < 64
    edge16 = (lane16 < 2) | (lane16 >= 126)
    for t in range(0, count, 2):
        ts = [t, min(t + 1, count - 1)]
        both = [cat(*[q(u, j, 8 * xg) for u in ts]) for j in range(J)]
        outer = cat(*[pltpu.roll(edges[u // 4], (254 - place(u, xg)) % 128, 1) for u in ts]).astype(bf16)
        high = [a.astype(bf16) for a in both]
        for j in range(J):
            left = outer if j == 0 else high[j - 1]
            right = outer if j == J - 1 else high[j + 1]
            low = (both[j] - high[j].astype(f32)).astype(bf16)
            second = jnp.where(edge16, jnp.where(half16, right, left), low)
            lhs = jnp.concatenate([high[j], second], 1)
            for m in range(2):
                pltpu.matmul_acc_lhs(accs[m][base], lhs)
            base += 1


def finish_row(q, cf, sub, accs, base, put, count, xg, packed):
    for t in range(0, count, 2):
        new = {}
        for j in range(J):
            c = [cf[j, xg, 7 * sub + k] for k in range(7)]
            upper, lower = (pltpu.matmul_pop(accs[m][base]) for m in range(2))
            base += 1
            for u in range(min(2, count - t)):
                r = slice(8 * u, 8 * u + 8)
                x = [q(t + u, j, 8 * xg + d) for d in (-2, -1, 0, 1, 2)]
                s = (c[0] * x[0] + c[1] * x[1]) + (c[2] * x[2] + c[3] * x[3])
                v = c[4] * x[4] + c[5] * jnp.where(c[5] < 0, upper[r, :128], upper[r, 128:])
                v = v + c[6] * jnp.where(c[6] > 0, lower[r, :128], lower[r, 128:])
                new[u, j] = s + v
                put(t + u, j, xg, new[u, j])
        if packed is not None:
            for u in range(min(2, count - t)):
                k = (t + u) // 4
                packed[k] = pack_edges(packed[k], t + u, xg, new[u, 0], new[u, J - 1])


def advance(q, cf, sub, accs, edges, put, count, packed):
    issue_row(q, accs, 0, edges, count, 0)
    for xg in range(8):
        if xg < 7:
            issue_row(q, accs, (xg + 1) % 2 * SET, edges, count, xg + 1)
        finish_row(q, cf, sub, accs, xg % 2 * SET, put, count, xg, packed)
    return packed


def with_accumulators(body):
    n = 2 * SET
    pl.run_scoped(lambda *a: body((a[:n], a[n:])), *[pltpu.ACC(i // n)((16, 256), f32) for i in range(2 * n)])


def total(items):
    out = items[0]
    for item in items[1:]:
        out = out + item
    return out


def flag(condition):
    return jnp.where(condition, 1, 0).astype(jnp.int32)


def water_places(water_ref):
    ids = [water_ref[w] for w in range(NW)]
    halves = [i // NT for i in ids]
    ranks = [total([jnp.int32(0)] + [flag(halves[v] == halves[w]) for v in range(w)]) for w in range(NW)]
    ranks = [jnp.minimum(r, PW - 1) for r in ranks]
    return ids, halves, ranks


def first_kernel(*refs):
    with_accumulators(lambda accs: first_body(accs, *refs))


def first_body(
    accs,
    slot_ref, water_ref, mass_hbm, flux_hbm, w_hbm, tracers,
    q1, cf_out, lo2, hi2, zl2, zr2, arrived,
    mass_ref, flux_ref, w_ref, cf, q0, q1v, z1, up1, dn1, lo1, hi1, z0, zl1, zr1, up2, dn2, tsend, trecv, xsend, xrecv,
    mass, fx, fy, qw, qw1, upw, dnw, low, hiw, zw, zlw, zrw, q2w, wsend,
    load_sem, tile_ssem, tile_rsem, row_ssem, row_rsem, halo_ssem, halo_rsem,
    next_ssem, next_rsem, wh_ssem, wh_rsem, ws_sem, wr_sem, out_sem, field_sem,
):
    grp, gx, gy = lax.axis_index("grp"), lax.axis_index("gx"), lax.axis_index("gy")
    me = (grp * NX + gx) * NY + gy
    pos = grp * NY + gy
    lane = lanes()

    def at(x, p):
        return {"grp": p // NY, "gx": x, "gy": lax.rem(p, NY)}

    def peer(k):
        return lax.rem(pos + k, GROUP)

    fields = [
        pltpu.make_async_copy(a, b, field_sem.at[n])
        for n, (a, b) in enumerate(((mass_hbm, mass_ref), (flux_hbm, flux_ref), (w_hbm, w_ref)))
    ]
    for copy in fields:
        copy.start()

    def load(c, j):
        return pltpu.make_async_copy(
            tracers.at[pl.ds(c * T, T), :, pl.ds(128 * j, 128)],
            q0.at[pl.ds(c * T, T), j, pl.ds(8, 64), :],
            load_sem.at[c, j],
        )

    def start_load(c, _):
        for j in range(J):
            load(c, j).start()
        return 0

    lax.fori_loop(0, CH, start_load, 0)

    barrier = pltpu.get_barrier_semaphore()

    def greet(device):
        pl.semaphore_signal(barrier, inc=1, device_id=device, device_id_type=MESH)

    for k in range(1, GROUP):
        greet(at(gx, peer(k)))

    @pl.when(gx > 0)
    def _():
        for k in range(GROUP):
            greet(at(gx - 1, peer(k)))

    @pl.when(gx < NX - 1)
    def _():
        for k in range(GROUP):
            greet(at(gx + 1, peer(k)))

    for copy in fields:
        copy.wait()

    def held(c, only=None):
        choice = jnp.int32(0)
        for i in range(TPB) if only is None else (only,):
            g = slot_ref[(gx * NY + c) * TPB + i]
            choice = jnp.where(g // SLOTS == me, g % SLOTS, choice)
        return choice

    for c in range(NY):
        s = held(c)
        for j in range(J):
            cols = slice(128 * j, 128 * j + 128)
            tsend[c, pl.ds(16 * j, 16), :] = mass_ref[s, :, cols]
            tsend[c, pl.ds(48 + 16 * j, 16), :] = flux_ref[s, 0, :, cols]
            tsend[c, pl.ds(96 + 16 * j, 16), :] = flux_ref[s, 1, :, cols]
        if c > 0:
            b = held(c - 1)
            above = pltpu.roll(flux_ref[b, 1, pl.ds(8, 8), 256:384], 64, 1)
            tsend[c, pl.ds(144, 8), :] = jnp.where(lane < 64, above, flux_ref[b, 1, pl.ds(0, 8), 256:384])
        else:
            tsend[c, pl.ds(144, 8), :] = jnp.zeros((8, 128), f32)
        d = held(c, TPB - 1)
        xsend[c] = jnp.zeros((8, 128), f32)
        for j in range(J):
            xsend[c, pl.ds(j, 1), :] = flux_ref[d, 0, pl.ds(ROWS - 1, 1), 128 * j : 128 * j + 128]
    trecv[0] = tsend[gy]

    pl.semaphore_wait(barrier, GROUP - 1 + jnp.where(gx > 0, GROUP, 0) + jnp.where(gx < NX - 1, GROUP, 0))

    def tile_copy(k):
        return pltpu.make_async_remote_copy(
            src_ref=tsend.at[lax.rem(peer(k), NY)],
            dst_ref=trecv.at[k],
            send_sem=tile_ssem.at[k],
            recv_sem=tile_rsem.at[k],
            device_id=at(gx, peer(k)),
            device_id_type=MESH,
        )

    def row_copy(k):
        return pltpu.make_async_remote_copy(
            src_ref=xsend.at[lax.rem(peer(k), NY)],
            dst_ref=xrecv.at[k],
            send_sem=row_ssem.at[k],
            recv_sem=row_rsem.at[k],
            device_id=at(gx + 1, peer(k)),
            device_id_type=MESH,
        )

    for k in range(1, GROUP):
        tile_copy(k).start()

    @pl.when(gx < NX - 1)
    def _():
        for k in range(GROUP):
            row_copy(k).start()

    has = (gx < NX - 1, gx > 0, gy < NY - 1, gy > 0)
    get = (gx > 0, gx < NX - 1, gy > 0, gy < NY - 1)
    to = ({"gx": gx + 1}, {"gx": gx - 1}, {"gy": gy + 1}, {"gy": gy - 1})
    to = tuple({"grp": grp, "gx": gx, "gy": gy, **d} for d in to)

    def halo(d, src, dst, ssem, rsem):
        return pltpu.make_async_remote_copy(
            src_ref=src, dst_ref=dst, send_sem=ssem.at[d], recv_sem=rsem, device_id=to[d], device_id_type=MESH
        )

    sets1 = ((dn1, lo1), (up1, hi1), (z0, zl1), (z0, zr1))
    sets2 = ((dn2, lo2), (up2, hi2), (z1, zl2), (z1, zr2))
    setsw = ((dnw, low), (upw, hiw), (zw, zlw), (zw, zrw))

    def send_chunk(sets, c, ssem, rsem):
        for d, (src, dst) in enumerate(sets):

            @pl.when(has[d])
            def _(d=d, src=src, dst=dst):
                halo(d, src.at[c], dst.at[c], ssem, rsem.at[c, d] if rsem is halo_rsem else rsem.at[d]).start()

    def wait_sets(sets, ssem, rsem, receive):
        for d, (src, dst) in enumerate(sets):
            copy = halo(d, src, dst, ssem, rsem.at[0, d] if rsem is halo_rsem else rsem.at[d])

            @pl.when(get[d] if receive else has[d])
            def _(copy=copy):
                (copy.wait_recv if receive else copy.wait_send)()

    def wait_chunk(c):
        for d, (src, dst) in enumerate(sets1):

            @pl.when(get[d])
            def _(d=d, src=src, dst=dst):
                halo(d, src.at[c], dst.at[c], halo_ssem, halo_rsem.at[c, d]).wait_recv()

    def edge_rows(row):
        return [(t, j, (t * J + j) * 2) for t in range(row) for j in range(J)]

    def prepare(c, source, count):
        packed = [jnp.zeros((8, 128), f32)] * 2
        for t in range(count):
            for xg in range(8):
                packed[t // 4] = pack_edges(packed[t // 4], t, xg, source(t, 0, 8 * xg, 8), source(t, J - 1, 8 * xg, 8))
        for k in range(2):
            z0[c, k] = packed[k]
        for t, j, r in edge_rows(count):
            up1[c, pl.ds(r, 2), :] = source(t, j, 0, 2)
            dn1[c, pl.ds(r, 2), :] = source(t, j, 62, 2)
        send_chunk(sets1, c, halo_ssem, halo_rsem)

    def wait_load(c, _):
        for j in range(J):
            load(c, j).wait()
        return 0

    lax.fori_loop(0, CH, wait_load, 0)

    ids, halves, ranks = water_places(water_ref)
    for p in range(PW):
        tracer = jnp.int32(0)
        for w in range(NW):
            tracer = jnp.where((halves[w] == grp) & (ranks[w] == p), ids[w] % NT, tracer)
        for j in range(J):
            qw[p, j, pl.ds(8, 64), :] = q0[tracer, j, pl.ds(8, 64), :]
    prepare(CH, lambda t, j, r, n: qw[t, j, pl.ds(8 + r, n), :], PW)

    def prepare_chunk(c, _):
        prepare(c, lambda t, j, r, n: q0[c * T + t, j, pl.ds(8 + r, n), :], T)
        return 0

    lax.fori_loop(0, CH, prepare_chunk, 0)

    load_weights(w_ref, accs)

    for k in range(1, GROUP):
        tile_copy(k).wait_recv()

    @pl.when(gx > 0)
    def _():
        for k in range(GROUP):
            row_copy(k).wait_recv()

    def sender(tile):
        owner = slot_ref[tile] // SLOTS
        return lax.rem(pos + GROUP - (owner // (NX * NY) * NY + owner % NY), GROUP)

    base = (gx * NY + gy) * TPB
    left = []
    for i in range(TPB):
        k = sender(base + i)
        for j in range(J):
            mass[j, pl.ds(16 * i, 16), :] = trecv[k, pl.ds(16 * j, 16), :]
            fx[j, pl.ds(8 + 16 * i, 16), :] = trecv[k, pl.ds(48 + 16 * j, 16), :] * (1.0 / 12.0)
            fy[j, pl.ds(16 * i, 16), :] = trecv[k, pl.ds(96 + 16 * j, 16), :] * (1.0 / 12.0)
        k = sender(jnp.maximum(base - TPB, 0) + i)
        v = jnp.where(gy > 0, trecv[k, pl.ds(144, 8), :] * (1.0 / 12.0), 0.0)
        left += [v, pltpu.roll(v, 64, 1)]
    k = sender(jnp.maximum(base - NY * TPB, 0) + TPB - 1)
    for j in range(J):
        v = jnp.where(gx > 0, xrecv[k, pl.ds(j, 1), :] * (1.0 / 12.0), 0.0)
        fx[j, pl.ds(7, 1), :] = v
    for xg in range(8):
        moved = []
        for j in range(J):
            f = fx[j, pl.ds(8 + 8 * xg, 8), :]
            b = fx[j, pl.ds(7 + 8 * xg, 8), :]
            fp, fm, gp, gm = jnp.maximum(f, 0.0), jnp.minimum(f, 0.0), jnp.maximum(b, 0.0), jnp.minimum(b, 0.0)
            h = fy[j, pl.ds(8 * xg, 8), :]
            moved.append(pltpu.roll(h, 1, 1))
            last = pltpu.roll(left[xg], 1, 1) if j == 0 else moved[j - 1]
            h0 = jnp.where(lane == 0, last, moved[j])
            out = 6.0 * ((f - b) + (h - h0))
            m0 = mass[j, pl.ds(8 * xg, 8), :]
            centre = (5.0 * fp + 2.0 * fm) - (2.0 * gp + 5.0 * gm)
            for sub in range(2):
                m1 = m0 - out
                inv = 1.0 / m1
                for k, v in enumerate(
                    (-gp, fp + (5.0 * gp + 2.0 * gm), m0 - centre, -(2.0 * fp + 5.0 * fm) - gm, fm, -h, h0)
                ):
                    cf[j, xg, 7 * sub + k] = v * inv
                m0 = m1

    cf_copy = pltpu.make_async_copy(cf.at[:, :, pl.ds(7, 7)], cf_out, field_sem.at[0])
    cf_copy.start()
    wait_chunk(CH)
    def fill(dst, c, count, lo, hi):
        for t, j, r in edge_rows(count):
            dst(t, j, 6, jnp.where(get[0], lo[c, pl.ds(r, 2), :], 0.0))
            dst(t, j, 72, jnp.where(get[1], hi[c, pl.ds(r, 2), :], 0.0))

    def edge_terms(zl, zr, c):
        return [
            merge_edges(jnp.where(get[2], zl[c, k], 0.0), jnp.where(get[3], zr[c, k], 0.0)) for k in range(2)
        ]

    def put_qw(t, j, r, v):
        qw[t, j, pl.ds(r, 2), :] = v

    fill(put_qw, CH, PW, lo1, hi1)
    edges = edge_terms(zl1, zr1, CH)

    def put_qw1(t, j, xg, v):
        qw1[t, j, pl.ds(8 + 8 * xg, 8), :] = v

    packed = advance(
        lambda t, j, r: qw[t, j, pl.ds(8 + r, 8), :], cf, 0, accs, edges, put_qw1, PW,
        [jnp.zeros((8, 128), f32)] * 2,
    )
    for k in range(2):
        zw[0, k] = packed[k]
    for t, j, r in edge_rows(PW):
        upw[0, pl.ds(r, 2), :] = qw1[t, j, pl.ds(8, 2), :]
        dnw[0, pl.ds(r, 2), :] = qw1[t, j, pl.ds(70, 2), :]
    send_chunk(setsw, 0, wh_ssem, wh_rsem)

    def water_copy(k):
        return pltpu.make_async_remote_copy(
            src_ref=wsend.at[k],
            dst_ref=arrived.at[k],
            send_sem=ws_sem.at[k],
            recv_sem=wr_sem.at[k],
            device_id=at(gx, peer(k)),
            device_id_type=MESH,
        )

    def own_water():
        return pltpu.make_async_copy(wsend.at[0], arrived.at[0], ws_sem.at[0])

    def finish_water():
        wait_sets(setsw, wh_ssem, wh_rsem, True)

        def put_halo(t, j, r, v):
            qw1[t, j, pl.ds(r, 2), :] = v

        fill(put_halo, 0, PW, low, hiw)
        edges = edge_terms(zlw, zrw, 0)

        def put_q2(t, j, xg, v):
            q2w[xg // 2, t, j, pl.ds(8 * (xg % 2), 8), :] = v

        advance(
            lambda t, j, r: qw1[t, j, pl.ds(8 + r, 8), :], cf, 1, accs, edges, put_q2, PW, None
        )
        for k in range(GROUP):
            p = peer(k)
            owners = [slot_ref[base + i] // SLOTS for i in range(TPB)]
            tile = jnp.int32(0)
            for i in range(TPB):
                tile = jnp.where(owners[i] // (NX * NY) * NY + owners[i] % NY == p, i, tile)
            wsend[k] = q2w[tile]
        own_water().start()
        for k in range(1, GROUP):
            water_copy(k).start()

    def out_copy(c):
        return pltpu.make_async_copy(q1v.at[pl.ds(c * T, T)], q1.at[pl.ds(c * T, T)], out_sem.at[0])

    def chunk(c, _):
        def put_q0(t, j, r, v):
            q0[c * T + t, j, pl.ds(r, 2), :] = v

        wait_chunk(c)
        fill(put_q0, c, T, lo1, hi1)
        edges = edge_terms(zl1, zr1, c)

        def put_q1(t, j, xg, v):
            q1v[c * T + t, j, pl.ds(8 * xg, 8), :] = v

        packed = advance(
            lambda t, j, r: q0[c * T + t, j, pl.ds(8 + r, 8), :], cf, 0, accs, edges, put_q1, T,
            [jnp.zeros((8, 128), f32)] * 2,
        )
        for k in range(2):
            z1[c, k] = packed[k]
        for t, j, r in edge_rows(T):
            up2[c, pl.ds(r, 2), :] = q1v[c * T + t, j, pl.ds(0, 2), :]
            dn2[c, pl.ds(r, 2), :] = q1v[c * T + t, j, pl.ds(62, 2), :]
        out_copy(c).start()
        send_chunk(sets2, c, next_ssem, next_rsem)

        @pl.when(c == 1)
        def _():
            finish_water()

        return 0

    lax.fori_loop(0, CH, chunk, 0)

    cf_copy.wait()
    for k in range(1, GROUP):
        tile_copy(k).wait_send()

    @pl.when(gx < NX - 1)
    def _():
        for k in range(GROUP):
            row_copy(k).wait_send()

    wait_sets(sets1, halo_ssem, halo_rsem, False)
    wait_sets(setsw, wh_ssem, wh_rsem, False)
    wait_sets(sets2, next_ssem, next_rsem, False)
    wait_sets(sets2, next_ssem, next_rsem, True)
    pltpu.make_async_copy(q1v, q1, out_sem.at[0]).wait()
    own_water().wait()
    for k in range(1, GROUP):
        water_copy(k).wait()


def second_kernel(*refs):
    with_accumulators(lambda accs: second_body(accs, *refs))


def second_body(
    accs,
    slot_ref, water_ref, w_ref, cf_in, lo_in, hi_in, zl_in, zr_in, arrived_in, q1,
    out, water_out, cf, lo, hi, zl, zr, arrived, water, qb, ob, in_sem, out_sem, small_sem,
):
    grp, gx, gy = lax.axis_index("grp"), lax.axis_index("gx"), lax.axis_index("gy")
    me = (grp * NX + gx) * NY + gy
    pos = grp * NY + gy

    def load(c):
        return pltpu.make_async_copy(q1.at[pl.ds(c * T, T)], qb.at[pl.ds(c * T, T), :, pl.ds(8, 64), :], in_sem.at[c])

    def store(c):
        return pltpu.make_async_copy(ob.at[pl.ds(c * T, T)], out.at[pl.ds(c * T, T)], out_sem.at[c])

    def each(body):
        def step(c, _):
            body(c)
            return 0

        lax.fori_loop(0, CH, step, 0)

    small = [
        pltpu.make_async_copy(a, b, small_sem.at[n])
        for n, (a, b) in enumerate(
            ((cf_in, cf), (lo_in, lo), (hi_in, hi), (zl_in, zl), (zr_in, zr), (arrived_in, arrived), (water, water_out))
        )
    ]
    for copy in small[:5]:
        copy.start()
    each(lambda c: load(c).start())
    small[5].start()
    load_weights(w_ref, accs)

    def water_rows():
        small[5].wait()
        ids, halves, ranks = water_places(water_ref)
        for s in range(SLOTS):
            column, valid = jnp.int32(0), jnp.int32(0)
            for c in range(NY):
                for i in range(TPB):
                    match = slot_ref[(gx * NY + c) * TPB + i] == me * SLOTS + s
                    column = jnp.where(match, c, column)
                    valid = jnp.where(match, 1, valid)
            for w in range(NW):
                k = lax.rem(pos + GROUP - (halves[w] * NY + column), GROUP)
                for j in range(J):
                    water[s, w, :, 128 * j : 128 * j + 128] = jnp.where(valid > 0, arrived[k, ranks[w], j], 0.0)
        small[6].start()

    for copy in small[:5]:
        copy.wait()

    def chunk(c):
        load(c).wait()
        for t in range(T):
            for j in range(J):
                r = (t * J + j) * 2
                qb[c * T + t, j, pl.ds(6, 2), :] = jnp.where(gx > 0, lo[c, pl.ds(r, 2), :], 0.0)
                qb[c * T + t, j, pl.ds(72, 2), :] = jnp.where(gx < NX - 1, hi[c, pl.ds(r, 2), :], 0.0)
        edges = [
            merge_edges(jnp.where(gy > 0, zl[c, k], 0.0), jnp.where(gy < NY - 1, zr[c, k], 0.0)) for k in range(2)
        ]

        def put(t, j, xg, v):
            ob[c * T + t, pl.ds(8 * xg, 8), 128 * j : 128 * j + 128] = v

        advance(lambda t, j, r: qb[c * T + t, j, pl.ds(8 + r, 8), :], cf, 0, accs, edges, put, T, None)
        store(c).start()

        @pl.when(c == CH // 2)
        def _():
            water_rows()

    each(chunk)
    each(lambda c: store(c).wait())
    small[6].wait()


def per_device(tracers, dycore_air_mass, dycore_face_flux, tile_dycore_slot, water_idx):
    weights = jnp.asarray(stencil_weights(), bf16)
    smem = pl.BlockSpec(memory_space=pltpu.SMEM)
    vmem = pl.BlockSpec(memory_space=pltpu.VMEM)
    hbm = pl.BlockSpec(memory_space=pl.ANY)
    V, D = pltpu.VMEM, pltpu.SemaphoreType.DMA

    def S(*shape):
        return jax.ShapeDtypeStruct(shape, f32)

    edge, packs = (EDGE, 128), (2, 8, 128)
    scratch = [
        V((SLOTS, ROWS, J * 128), f32), V((SLOTS, 2, ROWS, J * 128), f32), V((256, 512), bf16), V((J, 8, 14, 8, 128), f32),
        V((NT, J, 80, 128), f32), V((NT, J, 64, 128), f32), V((CH, *packs), f32),
        V((CH + 1, *edge), f32), V((CH + 1, *edge), f32), V((CH + 1, *edge), f32), V((CH + 1, *edge), f32),
        V((CH + 1, *packs), f32), V((CH + 1, *packs), f32), V((CH + 1, *packs), f32),
        V((CH, *edge), f32), V((CH, *edge), f32),
        V((NY, 152, 128), f32), V((GROUP, 152, 128), f32), V((NY, 8, 128), f32), V((GROUP, 8, 128), f32),
        V((J, 64, 128), f32), V((J, 72, 128), f32), V((J, 64, 128), f32),
        V((PW, J, 80, 128), f32), V((PW, J, 80, 128), f32),
        V((1, *edge), f32), V((1, *edge), f32), V((1, *edge), f32), V((1, *edge), f32),
        V((1, *packs), f32), V((1, *packs), f32), V((1, *packs), f32),
        V((TPB, PW, J, ROWS, 128), f32), V((GROUP, PW, J, ROWS, 128), f32),
        D((CH, J)), D((GROUP,)), D((GROUP,)), D((GROUP,)), D((GROUP,)), D((4,)), D((CH + 1, 4)),
        D((4,)), D((4,)), D((4,)), D((4,)), D((GROUP,)), D((GROUP,)), D((1,)), D((3,)),
    ]
    q1, cf, lo, hi, zl, zr, arrived = pl.pallas_call(
        first_kernel,
        out_shape=(
            S(NT, J, 64, 128), S(J, 8, 7, 8, 128), S(CH, *edge), S(CH, *edge), S(CH, *packs), S(CH, *packs),
            S(GROUP, PW, J, ROWS, 128),
        ),
        in_specs=[smem, smem, hbm, hbm, hbm, hbm],
        out_specs=(hbm,) * 7,
        scratch_shapes=scratch,
        compiler_params=pltpu.CompilerParams(
            collective_id=0, has_side_effects=True, vmem_limit_bytes=60 * 2**20
        ),
        name="first_substep",
    )(tile_dycore_slot, water_idx, dycore_air_mass, dycore_face_flux, weights, tracers)
    return pl.pallas_call(
        second_kernel,
        out_shape=(S(NT, 64, J * 128), S(SLOTS, NW, ROWS, J * 128)),
        in_specs=[smem, smem, vmem] + [hbm] * 7,
        out_specs=(hbm, hbm),
        scratch_shapes=[
            V((J, 8, 7, 8, 128), f32), V((CH, *edge), f32), V((CH, *edge), f32), V((CH, *packs), f32), V((CH, *packs), f32),
            V((GROUP, PW, J, ROWS, 128), f32), V((SLOTS, NW, ROWS, J * 128), f32),
            V((NT, J, 80, 128), f32), V((NT, 64, J * 128), f32), D((CH,)), D((CH,)), D((7,)),
        ],
        compiler_params=pltpu.CompilerParams(
            vmem_limit_bytes=60 * 2**20
        ),
        name="second_substep",
    )(tile_dycore_slot, water_idx, weights, cf, lo, hi, zl, zr, arrived, q1)


def solution(mesh):
    return jax.shard_map(
        per_device,
        mesh=mesh,
        in_specs=(
            P("grp", "gx", "gy"),
            P(("grp", "gx", "gy"), None, None),
            P(("grp", "gx", "gy"), None, None, None),
            P(),
            P(),
        ),
        out_specs=(P("grp", "gx", "gy"), P(("grp", "gx", "gy"), None, None, None)),
        check_vma=False,
    )
```

```python
import jax
import jax.numpy as jnp
import numpy as np
from jax import lax
from jax.experimental import pallas as pl
from jax.experimental.pallas import tpu as pltpu
from jax.sharding import PartitionSpec as P

MESH = pl.DeviceIdType.MESH
f32 = jnp.float32
bf16 = jnp.bfloat16

NG, NX, NY = 2, 16, 4
GROUP = NG * NY
TPB = 4
SLOTS = 4
ROWS = 16
J = 3
T = 8
NT = 128
CH = NT // T
NW = 6
PW = 5
EDGE = T * J * 2
SET = T // 2 * J


def stencil_weights():
    w = np.zeros((256, 512), np.float32)
    for b, (shift, taps) in enumerate(
        (s, t) for s in (0, -1) for t in ({-1: -1, 0: 5, 1: 2}, {0: 2, 1: 5, 2: -1})
    ):
        for n in range(128):
            for d, v in taps.items():
                y = n + d + shift
                if 0 <= y < 128:
                    w[y, b * 128 + n] += v
                    if 2 <= y < 126:
                        w[128 + y, b * 128 + n] += v
                else:
                    w[(256 + y) if y < 0 else y, b * 128 + n] += v
    return w


def lanes():
    return lax.broadcasted_iota(jnp.int32, (8, 128), 1)


def cat(a, b):
    return jnp.concatenate([a, b], 0)


def place(t, xg):
    return 4 * ((t % 4) * 8 + xg)


def pack_edges(old, t, xg, first, last):
    m = place(t, xg)
    lane = lanes()
    mixed = pltpu.roll(jnp.where(lane < 64, first, last), (m + 2) % 128, 1)
    return jnp.where((lane >> 2) == m // 4, mixed, old)


def merge_edges(left, right):
    return jnp.where((lanes() & 3) < 2, left, right)


def load_weights(w_ref, accs):
    for m in range(2):
        pltpu.matmul_push_rhs(w_ref[:, 256 * m : 256 * m + 256], 0, m)
        pltpu.matmul_acc_lhs(accs[m][0], jnp.zeros((16, 256), bf16), load_staged_rhs=0)
        pltpu.matmul_pop(accs[m][0])


def issue_row(q, accs, base, edges, count, xg):
    lane16 = lax.broadcasted_iota(jnp.int32, (16, 128), 1)
    half16 = lane16 < 64
    edge16 = (lane16 < 2) | (lane16 >= 126)
    for t in range(0, count, 2):
        ts = [t, min(t + 1, count - 1)]
        both = [cat(*[q(u, j, 8 * xg) for u in ts]) for j in range(J)]
        outer = cat(*[pltpu.roll(edges[u // 4], (254 - place(u, xg)) % 128, 1) for u in ts]).astype(bf16)
        high = [a.astype(bf16) for a in both]
        for j in range(J):
            left = outer if j == 0 else high[j - 1]
            right = outer if j == J - 1 else high[j + 1]
            low = (both[j] - high[j].astype(f32)).astype(bf16)
            second = jnp.where(edge16, jnp.where(half16, right, left), low)
            lhs = jnp.concatenate([high[j], second], 1)
            for m in range(2):
                pltpu.matmul_acc_lhs(accs[m][base], lhs)
            base += 1


def finish_row(q, cf, sub, accs, base, put, count, xg, packed):
    for t in range(0, count, 2):
        new = {}
        for j in range(J):
            c = [cf[j, xg, 7 * sub + k] for k in range(7)]
            upper, lower = (pltpu.matmul_pop(accs[m][base]) for m in range(2))
            base += 1
            for u in range(min(2, count - t)):
                r = slice(8 * u, 8 * u + 8)
                x = [q(t + u, j, 8 * xg + d) for d in (-2, -1, 0, 1, 2)]
                s = (c[0] * x[0] + c[1] * x[1]) + (c[2] * x[2] + c[3] * x[3])
                v = c[4] * x[4] + c[5] * jnp.where(c[5] < 0, upper[r, :128], upper[r, 128:])
                v = v + c[6] * jnp.where(c[6] > 0, lower[r, :128], lower[r, 128:])
                new[u, j] = s + v
                put(t + u, j, xg, new[u, j])
        if packed is not None:
            for u in range(min(2, count - t)):
                k = (t + u) // 4
                packed[k] = pack_edges(packed[k], t + u, xg, new[u, 0], new[u, J - 1])


def advance(q, cf, sub, accs, edges, put, count, packed):
    issue_row(q, accs, 0, edges, count, 0)
    for xg in range(8):
        if xg < 7:
            issue_row(q, accs, (xg + 1) % 2 * SET, edges, count, xg + 1)
        finish_row(q, cf, sub, accs, xg % 2 * SET, put, count, xg, packed)
    return packed


def with_accumulators(body):
    n = 2 * SET
    pl.run_scoped(lambda *a: body((a[:n], a[n:])), *[pltpu.ACC(i // n)((16, 256), f32) for i in range(2 * n)])


def total(items):
    out = items[0]
    for item in items[1:]:
        out = out + item
    return out


def flag(condition):
    return jnp.where(condition, 1, 0).astype(jnp.int32)


def water_places(water_ref):
    ids = [water_ref[w] for w in range(NW)]
    halves = [i // NT for i in ids]
    ranks = [total([jnp.int32(0)] + [flag(halves[v] == halves[w]) for v in range(w)]) for w in range(NW)]
    ranks = [jnp.minimum(r, PW - 1) for r in ranks]
    return ids, halves, ranks


def first_kernel(*refs):
    with_accumulators(lambda accs: first_body(accs, *refs))


def first_body(
    accs,
    slot_ref, water_ref, mass_hbm, flux_hbm, w_hbm, tracers,
    q1, cf_out, lo2, hi2, zl2, zr2, arrived,
    mass_ref, flux_ref, w_ref, cf, q0, q1v, z1, up1, dn1, lo1, hi1, z0, zl1, zr1, up2, dn2, tsend, trecv, xsend, xrecv,
    mass, fx, fy, qw, qw1, upw, dnw, low, hiw, zw, zlw, zrw, q2w, wsend,
    load_sem, tile_ssem, tile_rsem, row_ssem, row_rsem, halo_ssem, halo_rsem,
    next_ssem, next_rsem, wh_ssem, wh_rsem, ws_sem, wr_sem, out_sem, field_sem,
):
    grp, gx, gy = lax.axis_index("grp"), lax.axis_index("gx"), lax.axis_index("gy")
    me = (grp * NX + gx) * NY + gy
    pos = grp * NY + gy
    lane = lanes()

    def at(x, p):
        return {"grp": p // NY, "gx": x, "gy": lax.rem(p, NY)}

    def peer(k):
        return lax.rem(pos + k, GROUP)

    fields = [
        pltpu.make_async_copy(a, b, field_sem.at[n])
        for n, (a, b) in enumerate(((mass_hbm, mass_ref), (flux_hbm, flux_ref), (w_hbm, w_ref)))
    ]
    for copy in fields:
        copy.start()

    def load(c, j):
        return pltpu.make_async_copy(
            tracers.at[pl.ds(c * T, T), :, pl.ds(128 * j, 128)],
            q0.at[pl.ds(c * T, T), j, pl.ds(8, 64), :],
            load_sem.at[c, j],
        )

    def start_load(c, _):
        for j in range(J):
            load(c, j).start()
        return 0


    barrier = pltpu.get_barrier_semaphore()

    def greet(device):
        pl.semaphore_signal(barrier, inc=1, device_id=device, device_id_type=MESH)

    for k in range(1, GROUP):
        greet(at(gx, peer(k)))

    @pl.when(gx > 0)
    def _():
        for k in range(GROUP):
            greet(at(gx - 1, peer(k)))

    @pl.when(gx < NX - 1)
    def _():
        for k in range(GROUP):
            greet(at(gx + 1, peer(k)))

    for copy in fields:
        copy.wait()

    def held(c, only=None):
        choice = jnp.int32(0)
        for i in range(TPB) if only is None else (only,):
            g = slot_ref[(gx * NY + c) * TPB + i]
            choice = jnp.where(g // SLOTS == me, g % SLOTS, choice)
        return choice

    for c in range(NY):
        s = held(c)
        for j in range(J):
            cols = slice(128 * j, 128 * j + 128)
            tsend[c, pl.ds(16 * j, 16), :] = mass_ref[s, :, cols]
            tsend[c, pl.ds(48 + 16 * j, 16), :] = flux_ref[s, 0, :, cols]
            tsend[c, pl.ds(96 + 16 * j, 16), :] = flux_ref[s, 1, :, cols]
        if c > 0:
            b = held(c - 1)
            above = pltpu.roll(flux_ref[b, 1, pl.ds(8, 8), 256:384], 64, 1)
            tsend[c, pl.ds(144, 8), :] = jnp.where(lane < 64, above, flux_ref[b, 1, pl.ds(0, 8), 256:384])
        else:
            tsend[c, pl.ds(144, 8), :] = jnp.zeros((8, 128), f32)
        d = held(c, TPB - 1)
        xsend[c] = jnp.zeros((8, 128), f32)
        for j in range(J):
            xsend[c, pl.ds(j, 1), :] = flux_ref[d, 0, pl.ds(ROWS - 1, 1), 128 * j : 128 * j + 128]
    trecv[0] = tsend[gy]

    lax.fori_loop(0, CH, start_load, 0)
    pl.semaphore_wait(barrier, GROUP - 1 + jnp.where(gx > 0, GROUP, 0) + jnp.where(gx < NX - 1, GROUP, 0))

    def tile_copy(k):
        return pltpu.make_async_remote_copy(
            src_ref=tsend.at[lax.rem(peer(k), NY)],
            dst_ref=trecv.at[k],
            send_sem=tile_ssem.at[k],
            recv_sem=tile_rsem.at[k],
            device_id=at(gx, peer(k)),
            device_id_type=MESH,
        )

    def row_copy(k):
        return pltpu.make_async_remote_copy(
            src_ref=xsend.at[lax.rem(peer(k), NY)],
            dst_ref=xrecv.at[k],
            send_sem=row_ssem.at[k],
            recv_sem=row_rsem.at[k],
            device_id=at(gx + 1, peer(k)),
            device_id_type=MESH,
        )

    for k in range(1, GROUP):
        tile_copy(k).start()

    @pl.when(gx < NX - 1)
    def _():
        for k in range(GROUP):
            row_copy(k).start()

    has = (gx < NX - 1, gx > 0, gy < NY - 1, gy > 0)
    get = (gx > 0, gx < NX - 1, gy > 0, gy < NY - 1)
    to = ({"gx": gx + 1}, {"gx": gx - 1}, {"gy": gy + 1}, {"gy": gy - 1})
    to = tuple({"grp": grp, "gx": gx, "gy": gy, **d} for d in to)

    def halo(d, src, dst, ssem, rsem):
        return pltpu.make_async_remote_copy(
            src_ref=src, dst_ref=dst, send_sem=ssem.at[d], recv_sem=rsem, device_id=to[d], device_id_type=MESH
        )

    sets1 = ((dn1, lo1), (up1, hi1), (z0, zl1), (z0, zr1))
    sets2 = ((dn2, lo2), (up2, hi2), (z1, zl2), (z1, zr2))
    setsw = ((dnw, low), (upw, hiw), (zw, zlw), (zw, zrw))

    def send_chunk(sets, c, ssem, rsem):
        for d, (src, dst) in enumerate(sets):

            @pl.when(has[d])
            def _(d=d, src=src, dst=dst):
                halo(d, src.at[c], dst.at[c], ssem, rsem.at[c, d] if rsem is halo_rsem else rsem.at[d]).start()

    def wait_sets(sets, ssem, rsem, receive):
        for d, (src, dst) in enumerate(sets):
            copy = halo(d, src, dst, ssem, rsem.at[0, d] if rsem is halo_rsem else rsem.at[d])

            @pl.when(get[d] if receive else has[d])
            def _(copy=copy):
                (copy.wait_recv if receive else copy.wait_send)()

    def wait_chunk(c):
        for d, (src, dst) in enumerate(sets1):

            @pl.when(get[d])
            def _(d=d, src=src, dst=dst):
                halo(d, src.at[c], dst.at[c], halo_ssem, halo_rsem.at[c, d]).wait_recv()

    def edge_rows(row):
        return [(t, j, (t * J + j) * 2) for t in range(row) for j in range(J)]

    def prepare(c, source, count):
        packed = [jnp.zeros((8, 128), f32)] * 2
        for t in range(count):
            for xg in range(8):
                packed[t // 4] = pack_edges(packed[t // 4], t, xg, source(t, 0, 8 * xg, 8), source(t, J - 1, 8 * xg, 8))
        for k in range(2):
            z0[c, k] = packed[k]
        for t, j, r in edge_rows(count):
            up1[c, pl.ds(r, 2), :] = source(t, j, 0, 2)
            dn1[c, pl.ds(r, 2), :] = source(t, j, 62, 2)
        send_chunk(sets1, c, halo_ssem, halo_rsem)

    def wait_load(c, _):
        for j in range(J):
            load(c, j).wait()
        return 0

    lax.fori_loop(0, CH, wait_load, 0)

    ids, halves, ranks = water_places(water_ref)
    for p in range(PW):
        tracer = jnp.int32(0)
        for w in range(NW):
            tracer = jnp.where((halves[w] == grp) & (ranks[w] == p), ids[w] % NT, tracer)
        for j in range(J):
            qw[p, j, pl.ds(8, 64), :] = q0[tracer, j, pl.ds(8, 64), :]
    prepare(CH, lambda t, j, r, n: qw[t, j, pl.ds(8 + r, n), :], PW)

    def prepare_chunk(c, _):
        prepare(c, lambda t, j, r, n: q0[c * T + t, j, pl.ds(8 + r, n), :], T)
        return 0

    lax.fori_loop(0, CH, prepare_chunk, 0)

    load_weights(w_ref, accs)

    for k in range(1, GROUP):
        tile_copy(k).wait_recv()

    @pl.when(gx > 0)
    def _():
        for k in range(GROUP):
            row_copy(k).wait_recv()

    def sender(tile):
        owner = slot_ref[tile] // SLOTS
        return lax.rem(pos + GROUP - (owner // (NX * NY) * NY + owner % NY), GROUP)

    base = (gx * NY + gy) * TPB
    left = []
    for i in range(TPB):
        k = sender(base + i)
        for j in range(J):
            mass[j, pl.ds(16 * i, 16), :] = trecv[k, pl.ds(16 * j, 16), :]
            fx[j, pl.ds(8 + 16 * i, 16), :] = trecv[k, pl.ds(48 + 16 * j, 16), :] * (1.0 / 12.0)
            fy[j, pl.ds(16 * i, 16), :] = trecv[k, pl.ds(96 + 16 * j, 16), :] * (1.0 / 12.0)
        k = sender(jnp.maximum(base - TPB, 0) + i)
        v = jnp.where(gy > 0, trecv[k, pl.ds(144, 8), :] * (1.0 / 12.0), 0.0)
        left += [v, pltpu.roll(v, 64, 1)]
    k = sender(jnp.maximum(base - NY * TPB, 0) + TPB - 1)
    for j in range(J):
        v = jnp.where(gx > 0, xrecv[k, pl.ds(j, 1), :] * (1.0 / 12.0), 0.0)
        fx[j, pl.ds(7, 1), :] = v
    for xg in range(8):
        moved = []
        for j in range(J):
            f = fx[j, pl.ds(8 + 8 * xg, 8), :]
            b = fx[j, pl.ds(7 + 8 * xg, 8), :]
            fp, fm, gp, gm = jnp.maximum(f, 0.0), jnp.minimum(f, 0.0), jnp.maximum(b, 0.0), jnp.minimum(b, 0.0)
            h = fy[j, pl.ds(8 * xg, 8), :]
            moved.append(pltpu.roll(h, 1, 1))
            last = pltpu.roll(left[xg], 1, 1) if j == 0 else moved[j - 1]
            h0 = jnp.where(lane == 0, last, moved[j])
            out = 6.0 * ((f - b) + (h - h0))
            m0 = mass[j, pl.ds(8 * xg, 8), :]
            centre = (5.0 * fp + 2.0 * fm) - (2.0 * gp + 5.0 * gm)
            for sub in range(2):
                m1 = m0 - out
                inv = 1.0 / m1
                for k, v in enumerate(
                    (-gp, fp + (5.0 * gp + 2.0 * gm), m0 - centre, -(2.0 * fp + 5.0 * fm) - gm, fm, -h, h0)
                ):
                    cf[j, xg, 7 * sub + k] = v * inv
                m0 = m1

    cf_copy = pltpu.make_async_copy(cf.at[:, :, pl.ds(7, 7)], cf_out, field_sem.at[0])
    cf_copy.start()
    wait_chunk(CH)
    def fill(dst, c, count, lo, hi):
        for t, j, r in edge_rows(count):
            dst(t, j, 6, jnp.where(get[0], lo[c, pl.ds(r, 2), :], 0.0))
            dst(t, j, 72, jnp.where(get[1], hi[c, pl.ds(r, 2), :], 0.0))

    def edge_terms(zl, zr, c):
        return [
            merge_edges(jnp.where(get[2], zl[c, k], 0.0), jnp.where(get[3], zr[c, k], 0.0)) for k in range(2)
        ]

    def put_qw(t, j, r, v):
        qw[t, j, pl.ds(r, 2), :] = v

    fill(put_qw, CH, PW, lo1, hi1)
    edges = edge_terms(zl1, zr1, CH)

    def put_qw1(t, j, xg, v):
        qw1[t, j, pl.ds(8 + 8 * xg, 8), :] = v

    packed = advance(
        lambda t, j, r: qw[t, j, pl.ds(8 + r, 8), :], cf, 0, accs, edges, put_qw1, PW,
        [jnp.zeros((8, 128), f32)] * 2,
    )
    for k in range(2):
        zw[0, k] = packed[k]
    for t, j, r in edge_rows(PW):
        upw[0, pl.ds(r, 2), :] = qw1[t, j, pl.ds(8, 2), :]
        dnw[0, pl.ds(r, 2), :] = qw1[t, j, pl.ds(70, 2), :]
    send_chunk(setsw, 0, wh_ssem, wh_rsem)

    def water_copy(k):
        return pltpu.make_async_remote_copy(
            src_ref=wsend.at[k],
            dst_ref=arrived.at[k],
            send_sem=ws_sem.at[k],
            recv_sem=wr_sem.at[k],
            device_id=at(gx, peer(k)),
            device_id_type=MESH,
        )

    def own_water():
        return pltpu.make_async_copy(wsend.at[0], arrived.at[0], ws_sem.at[0])

    def finish_water():
        wait_sets(setsw, wh_ssem, wh_rsem, True)

        def put_halo(t, j, r, v):
            qw1[t, j, pl.ds(r, 2), :] = v

        fill(put_halo, 0, PW, low, hiw)
        edges = edge_terms(zlw, zrw, 0)

        def put_q2(t, j, xg, v):
            q2w[xg // 2, t, j, pl.ds(8 * (xg % 2), 8), :] = v

        advance(
            lambda t, j, r: qw1[t, j, pl.ds(8 + r, 8), :], cf, 1, accs, edges, put_q2, PW, None
        )
        for k in range(GROUP):
            p = peer(k)
            owners = [slot_ref[base + i] // SLOTS for i in range(TPB)]
            tile = jnp.int32(0)
            for i in range(TPB):
                tile = jnp.where(owners[i] // (NX * NY) * NY + owners[i] % NY == p, i, tile)
            wsend[k] = q2w[tile]
        own_water().start()
        for k in range(1, GROUP):
            water_copy(k).start()

    def out_copy(c):
        return pltpu.make_async_copy(q1v.at[pl.ds(c * T, T)], q1.at[pl.ds(c * T, T)], out_sem.at[0])

    def chunk(c, _):
        def put_q0(t, j, r, v):
            q0[c * T + t, j, pl.ds(r, 2), :] = v

        wait_chunk(c)
        fill(put_q0, c, T, lo1, hi1)
        edges = edge_terms(zl1, zr1, c)

        def put_q1(t, j, xg, v):
            q1v[c * T + t, j, pl.ds(8 * xg, 8), :] = v

        packed = advance(
            lambda t, j, r: q0[c * T + t, j, pl.ds(8 + r, 8), :], cf, 0, accs, edges, put_q1, T,
            [jnp.zeros((8, 128), f32)] * 2,
        )
        for k in range(2):
            z1[c, k] = packed[k]
        for t, j, r in edge_rows(T):
            up2[c, pl.ds(r, 2), :] = q1v[c * T + t, j, pl.ds(0, 2), :]
            dn2[c, pl.ds(r, 2), :] = q1v[c * T + t, j, pl.ds(62, 2), :]
        out_copy(c).start()
        send_chunk(sets2, c, next_ssem, next_rsem)

        @pl.when(c == 1)
        def _():
            finish_water()

        return 0

    lax.fori_loop(0, CH, chunk, 0)

    cf_copy.wait()
    for k in range(1, GROUP):
        tile_copy(k).wait_send()

    @pl.when(gx < NX - 1)
    def _():
        for k in range(GROUP):
            row_copy(k).wait_send()

    wait_sets(sets1, halo_ssem, halo_rsem, False)
    wait_sets(setsw, wh_ssem, wh_rsem, False)
    wait_sets(sets2, next_ssem, next_rsem, False)
    wait_sets(sets2, next_ssem, next_rsem, True)
    pltpu.make_async_copy(q1v, q1, out_sem.at[0]).wait()
    own_water().wait()
    for k in range(1, GROUP):
        water_copy(k).wait()


def second_kernel(*refs):
    with_accumulators(lambda accs: second_body(accs, *refs))


def second_body(
    accs,
    slot_ref, water_ref, w_ref, cf_in, lo_in, hi_in, zl_in, zr_in, arrived_in, q1,
    out, water_out, cf, lo, hi, zl, zr, arrived, water, qb, ob, in_sem, out_sem, small_sem,
):
    grp, gx, gy = lax.axis_index("grp"), lax.axis_index("gx"), lax.axis_index("gy")
    me = (grp * NX + gx) * NY + gy
    pos = grp * NY + gy

    def load(c):
        return pltpu.make_async_copy(q1.at[pl.ds(c * T, T)], qb.at[pl.ds(c * T, T), :, pl.ds(8, 64), :], in_sem.at[c])

    def store(c):
        return pltpu.make_async_copy(ob.at[pl.ds(c * T, T)], out.at[pl.ds(c * T, T)], out_sem.at[c])

    def each(body):
        def step(c, _):
            body(c)
            return 0

        lax.fori_loop(0, CH, step, 0)

    small = [
        pltpu.make_async_copy(a, b, small_sem.at[n])
        for n, (a, b) in enumerate(
            ((cf_in, cf), (lo_in, lo), (hi_in, hi), (zl_in, zl), (zr_in, zr), (arrived_in, arrived), (water, water_out))
        )
    ]
    for copy in small[:5]:
        copy.start()
    each(lambda c: load(c).start())
    small[5].start()
    load_weights(w_ref, accs)

    def water_rows():
        small[5].wait()
        ids, halves, ranks = water_places(water_ref)
        for s in range(SLOTS):
            column, valid = jnp.int32(0), jnp.int32(0)
            for c in range(NY):
                for i in range(TPB):
                    match = slot_ref[(gx * NY + c) * TPB + i] == me * SLOTS + s
                    column = jnp.where(match, c, column)
                    valid = jnp.where(match, 1, valid)
            for w in range(NW):
                k = lax.rem(pos + GROUP - (halves[w] * NY + column), GROUP)
                for j in range(J):
                    water[s, w, :, 128 * j : 128 * j + 128] = jnp.where(valid > 0, arrived[k, ranks[w], j], 0.0)
        small[6].start()

    for copy in small[:5]:
        copy.wait()

    def chunk(c):
        load(c).wait()
        for t in range(T):
            for j in range(J):
                r = (t * J + j) * 2
                qb[c * T + t, j, pl.ds(6, 2), :] = jnp.where(gx > 0, lo[c, pl.ds(r, 2), :], 0.0)
                qb[c * T + t, j, pl.ds(72, 2), :] = jnp.where(gx < NX - 1, hi[c, pl.ds(r, 2), :], 0.0)
        edges = [
            merge_edges(jnp.where(gy > 0, zl[c, k], 0.0), jnp.where(gy < NY - 1, zr[c, k], 0.0)) for k in range(2)
        ]

        def put(t, j, xg, v):
            ob[c * T + t, pl.ds(8 * xg, 8), 128 * j : 128 * j + 128] = v

        advance(lambda t, j, r: qb[c * T + t, j, pl.ds(8 + r, 8), :], cf, 0, accs, edges, put, T, None)
        store(c).start()

        @pl.when(c == CH // 2)
        def _():
            water_rows()

    each(chunk)
    each(lambda c: store(c).wait())
    small[6].wait()


def per_device(tracers, dycore_air_mass, dycore_face_flux, tile_dycore_slot, water_idx):
    weights = jnp.asarray(stencil_weights(), bf16)
    smem = pl.BlockSpec(memory_space=pltpu.SMEM)
    vmem = pl.BlockSpec(memory_space=pltpu.VMEM)
    hbm = pl.BlockSpec(memory_space=pl.ANY)
    V, D = pltpu.VMEM, pltpu.SemaphoreType.DMA

    def S(*shape):
        return jax.ShapeDtypeStruct(shape, f32)

    edge, packs = (EDGE, 128), (2, 8, 128)
    scratch = [
        V((SLOTS, ROWS, J * 128), f32), V((SLOTS, 2, ROWS, J * 128), f32), V((256, 512), bf16), V((J, 8, 14, 8, 128), f32),
        V((NT, J, 80, 128), f32), V((NT, J, 64, 128), f32), V((CH, *packs), f32),
        V((CH + 1, *edge), f32), V((CH + 1, *edge), f32), V((CH + 1, *edge), f32), V((CH + 1, *edge), f32),
        V((CH + 1, *packs), f32), V((CH + 1, *packs), f32), V((CH + 1, *packs), f32),
        V((CH, *edge), f32), V((CH, *edge), f32),
        V((NY, 152, 128), f32), V((GROUP, 152, 128), f32), V((NY, 8, 128), f32), V((GROUP, 8, 128), f32),
        V((J, 64, 128), f32), V((J, 72, 128), f32), V((J, 64, 128), f32),
        V((PW, J, 80, 128), f32), V((PW, J, 80, 128), f32),
        V((1, *edge), f32), V((1, *edge), f32), V((1, *edge), f32), V((1, *edge), f32),
        V((1, *packs), f32), V((1, *packs), f32), V((1, *packs), f32),
        V((TPB, PW, J, ROWS, 128), f32), V((GROUP, PW, J, ROWS, 128), f32),
        D((CH, J)), D((GROUP,)), D((GROUP,)), D((GROUP,)), D((GROUP,)), D((4,)), D((CH + 1, 4)),
        D((4,)), D((4,)), D((4,)), D((4,)), D((GROUP,)), D((GROUP,)), D((1,)), D((3,)),
    ]
    q1, cf, lo, hi, zl, zr, arrived = pl.pallas_call(
        first_kernel,
        out_shape=(
            S(NT, J, 64, 128), S(J, 8, 7, 8, 128), S(CH, *edge), S(CH, *edge), S(CH, *packs), S(CH, *packs),
            S(GROUP, PW, J, ROWS, 128),
        ),
        in_specs=[smem, smem, hbm, hbm, hbm, hbm],
        out_specs=(hbm,) * 7,
        scratch_shapes=scratch,
        compiler_params=pltpu.CompilerParams(
            collective_id=0,
            has_side_effects=True,
            vmem_limit_bytes=60 * 2**20,
        ),
        name="first_substep",
    )(tile_dycore_slot, water_idx, dycore_air_mass, dycore_face_flux, weights, tracers)
    return pl.pallas_call(
        second_kernel,
        out_shape=(S(NT, 64, J * 128), S(SLOTS, NW, ROWS, J * 128)),
        in_specs=[smem, smem, vmem] + [hbm] * 7,
        out_specs=(hbm, hbm),
        scratch_shapes=[
            V((J, 8, 7, 8, 128), f32), V((CH, *edge), f32), V((CH, *edge), f32), V((CH, *packs), f32), V((CH, *packs), f32),
            V((GROUP, PW, J, ROWS, 128), f32), V((SLOTS, NW, ROWS, J * 128), f32),
            V((NT, J, 80, 128), f32), V((NT, 64, J * 128), f32), D((CH,)), D((CH,)), D((7,)),
        ],
        compiler_params=pltpu.CompilerParams(
            vmem_limit_bytes=60 * 2**20
        ),
        name="second_substep",
    )(tile_dycore_slot, water_idx, weights, cf, lo, hi, zl, zr, arrived, q1)


def solution(mesh):
    return jax.shard_map(
        per_device,
        mesh=mesh,
        in_specs=(
            P("grp", "gx", "gy"),
            P(("grp", "gx", "gy"), None, None),
            P(("grp", "gx", "gy"), None, None, None),
            P(),
            P(),
        ),
        out_specs=(P("grp", "gx", "gy"), P(("grp", "gx", "gy"), None, None, None)),
        check_vma=False,
    )
```
